32 devices in a mesh: row: 8 (over y, x, core), col: 4 (over z).
Axes of the slice: x: 2, y: 2, z: 4, core: 2. Of those that a mesh axis runs over, the one named last changes fastest.
Arguments:
- sequence: bfloat16 [32768, 1536], P(('row', 'col')), may hold values from -6 to 6
- filter_weight: bfloat16 [3, 1536, 1536], replicated, may hold values from -0.09375 to 0.09375
- pair_proj: bfloat16 [1536, 256], replicated, may hold values from -0.15625 to 0.15625
- pair_out: bfloat16 [128, 128], replicated, may hold values from -0.5 to 0.5
- donor_w: bfloat16 [1536, 128], replicated, may hold values from -0.15625 to 0.15625
- donor_pos: int32 [8192], P(('row', 'col')), may hold values from 0 to 1023
- acceptor_bin: int32 [8192], P(('row', 'col')), may hold values from 0 to 255, as said below
Outputs:
- pair: bfloat16 [256, 256, 128], P('row', 'col')
- junctions: bfloat16 [8192, 128], P(('row', 'col'))
The draws below stay inside these ranges and needn't reach their ends.
Inputs may be any that keep to these rules, and one draw needn't show every extreme that they name: Among the 256 junctions of one device at most 64 have acceptor_bin in any one block of 64 pair columns; on every device some block holds exactly 64.
All inputs are finite; a program needn't handle non-finite values.
Results may differ from the reference program's by a relative error of at most 0.013.
Values may be sent and summed in bfloat16 or wider, within the bound.
A program may use at most 128 MiB of HBM per device.

```python
import jax
import jax.numpy as jnp
from jax import lax

D = 1536
PCH = 128
ROWS_DEV = 1024
DILATION_STEP = 32
POOL = 128
JUNC_DEV = 256
CAP = 64
SEQ = 32768
P_SIZE = 256
PC = 64
SLOTS = 256
NJ = 8192
JROWS = 8192
N_COL = 4
DEVICES = 32


def draw_acceptor_bin(key, part):
    slot_total_count = N_COL * CAP
    key_hot, key_forced, key_jitter, key_within = jax.random.split(key, 4)
    hotness_level = jax.random.randint(key_hot, (N_COL,), 0, 4)
    forced_choice = jax.random.randint(key_forced, (DEVICES,), 0, N_COL)
    random_noise = jax.random.randint(key_jitter, (DEVICES, slot_total_count), 0, 4096)
    group_labels = jnp.arange(slot_total_count, dtype=jnp.int32) // CAP
    extra_score = jnp.where(group_labels[None, :] == forced_choice[:, None], 1 << 20, 0)
    score_values = (random_noise + hotness_level[group_labels][None, :] * 4096 + extra_score) * slot_total_count + jnp.arange(slot_total_count, dtype=jnp.int32)[None, :]
    _, chosen = lax.top_k(score_values, JUNC_DEV)
    chosen_group = chosen // CAP
    within = jax.random.randint(key_within, (DEVICES, JUNC_DEV), 0, PC)
    return (chosen_group * PC + within).reshape(-1).astype(jnp.int32)


def with_ends(drawn, key, smallest, largest):
    shape = drawn.shape
    place = [jax.random.randint(jax.random.fold_in(key, axis), (), 0, shape[axis]) for axis in range(len(shape))]
    drawn = drawn.at[tuple(place)].set(smallest)
    longest = shape.index(max(shape))
    place[longest] = (place[longest] + 1) % shape[longest]
    return drawn.at[tuple(place)].set(largest)


def block_scale(stream_key, extent, cuts, least, top_value):
    def one(position, parts):
        steps = jax.random.uniform(jax.random.fold_in(jax.random.fold_in(stream_key, 6), position), (parts,), jnp.float32, least / len(cuts), top_value / len(cuts))
        return jnp.repeat(jnp.exp(steps), extent[position] // parts).reshape((-1,) + (1,) * (len(extent) - position - 1))

    factor_of = one(*cuts[0])
    for cut in cuts[1:]:
        factor_of = factor_of * one(*cut)
    return factor_of


def scatter_about(key, shape, scale, limit, cuts=(), kind=jnp.bfloat16):
    values = jax.random.normal(key, shape, jnp.float32) * scale
    if len(cuts) > 0:
        values = block_scale(key, shape, cuts, -0.22, 0.18) * values
    return jnp.clip(values, min=-limit, max=limit).astype(kind)


def setup_inputs(seed: int = 0) -> dict:
    keys = jax.random.split(jax.random.key(seed), 8)
    return {
        "sequence": scatter_about(keys[0], (SEQ, D), 1.0, 6.0, ((0, 32),)),
        "filter_weight": scatter_about(keys[1], (3, D, D), (3 * D) ** -0.5, 0.09375),
        "pair_proj": scatter_about(keys[2], (D, 2 * PCH), D ** -0.5, 0.15625),
        "pair_out": scatter_about(keys[3], (PCH, PCH), PCH ** -0.5, 0.5),
        "donor_w": scatter_about(keys[4], (D, PCH), D ** -0.5, 0.15625),
        "donor_pos": with_ends(jax.random.randint(keys[5], (NJ,), 0, ROWS_DEV), jax.random.fold_in(keys[5], 1), 0, ROWS_DEV - 1).astype(jnp.int32),
        "acceptor_bin": draw_acceptor_bin(jax.random.fold_in(keys[7], 71), 0),
    }


def reference(sequence, filter_weight, pair_proj, pair_out, donor_w, donor_pos, acceptor_bin):
    sequence_length = sequence.shape[0]
    padded_sequence = jnp.pad(sequence, ((DILATION_STEP, DILATION_STEP), (0, 0)))
    filtered_rows = jnp.dot(padded_sequence[0:sequence_length], filter_weight[0], preferred_element_type=jnp.float32)
    filtered_rows = filtered_rows + jnp.dot(padded_sequence[DILATION_STEP:DILATION_STEP + sequence_length], filter_weight[1], preferred_element_type=jnp.float32)
    filtered_rows = filtered_rows + jnp.dot(padded_sequence[2 * DILATION_STEP:2 * DILATION_STEP + sequence_length], filter_weight[2], preferred_element_type=jnp.float32)
    hidden = (sequence.astype(jnp.float32) + jax.nn.silu(filtered_rows)).astype(jnp.bfloat16)
    pooled = hidden.reshape(P_SIZE, POOL, D).astype(jnp.float32).mean(axis=1)
    normed = (pooled * lax.rsqrt(lax.optimization_barrier(jnp.mean(pooled * pooled, axis=-1, keepdims=True)) + 1e-06)).astype(jnp.bfloat16)
    projected = jnp.dot(normed, pair_proj, preferred_element_type=jnp.float32).astype(jnp.bfloat16)
    row_side = projected[:, :PCH].astype(jnp.float32)
    col_side = projected[:, PCH:].astype(jnp.float32)
    pair_hidden = jax.nn.relu(row_side[:, None, :] + col_side[None, :, :]).astype(jnp.bfloat16)
    pair = jnp.dot(pair_hidden.reshape(P_SIZE * P_SIZE, PCH), pair_out, preferred_element_type=jnp.float32)
    pair = pair.astype(jnp.bfloat16).reshape(P_SIZE, P_SIZE, PCH)
    sender = (jnp.arange(NJ) // JUNC_DEV).astype(jnp.int32)
    global_pos = (sender * ROWS_DEV + donor_pos).astype(jnp.int32)
    donor_rows = hidden[global_pos]
    donor_emb = jnp.dot(donor_rows, donor_w, preferred_element_type=jnp.float32).astype(jnp.bfloat16)
    looked = pair[global_pos // POOL, acceptor_bin]
    junction_value = jax.nn.relu(donor_emb.astype(jnp.float32) + looked.astype(jnp.float32)).astype(jnp.bfloat16)
    col_group = (acceptor_bin // PC).astype(jnp.int32)
    onehot = (col_group.reshape(DEVICES, JUNC_DEV)[:, :, None] == jnp.arange(N_COL, dtype=jnp.int32)[None, None, :]).astype(jnp.int32)
    earlier = jnp.cumsum(onehot, axis=1) - onehot
    slot_rank = lax.optimization_barrier(jnp.sum(earlier * onehot, axis=-1)).reshape(NJ).astype(jnp.int32)
    owner_index = sender // N_COL * N_COL + col_group
    target_row = (owner_index * SLOTS + sender % N_COL * CAP + slot_rank).astype(jnp.int32)
    junctions = jnp.zeros((JROWS, PCH), jnp.bfloat16).at[target_row].set(junction_value)
    return (pair, junctions)
```

```python
import functools

import jax
import jax.numpy as jnp
from jax import lax
from jax.experimental import pallas as pl
from jax.experimental.pallas import tpu as pltpu
from jax.sharding import PartitionSpec as P

DILATION_STEP = 32
POOL = 128
CAP = 64
LANES = 128
CHUNK = 512
MESH = pl.DeviceIdType.MESH
F32 = jnp.float32
BF16 = jnp.bfloat16


def dot(a, b):
    return jnp.dot(a, b, preferred_element_type=F32)


def dot_rows(a, b):
    return lax.dot_general(a, b, (((1,), (1,)), ((), ())), preferred_element_type=F32)


def hot(condition):
    return jnp.where(condition, 1.0, 0.0)


def trunk(
    n_row,
    n_col,
    x_hbm,
    w_hbm,
    proj_hbm,
    donor_hbm,
    pos_hbm,
    bin_hbm,
    rows_out,
    cols_out,
    emb_out,
    coord_out,
    xbuf,
    wbuf,
    mixed,
    parts,
    hidden,
    pooled,
    donor_emb,
    select,
    proj_ref,
    donor_ref,
    pos_list,
    bin_list,
    row_send,
    col_send,
    emb_send,
    x_sem,
    end_sem,
    w_sem,
    list_sem,
    halo_send_sem,
    halo_recv_sem,
    pos_send_sem,
    pos_recv_sem,
    bin_send_sem,
    bin_recv_sem,
    emb_send_sem,
    emb_recv_sem,
    row_send_sem,
    row_recv_sem,
    col_send_sem,
    col_recv_sem,
):
    rows, width = x_hbm.shape
    step = DILATION_STEP
    chunks = width // CHUNK
    bins = rows // POOL
    tile_cols = bins * n_row
    slots = n_col * CAP
    listed = pos_hbm.shape[1]
    count = n_row * n_col
    my_row = lax.axis_index("row")
    my_col = lax.axis_index("col")
    me = my_row * n_col + my_col

    groups = rows // (2 * step)
    quarter = groups // 4
    passes = (
        list(range(quarter, groups - quarter)),
        list(range(quarter)) + list(range(groups - quarter, groups)),
    )
    part_rows = len(passes[0]) * step

    def place(flat):
        return (flat // n_col, lax.rem(flat, n_col))

    def w_copy(tap, n):
        return pltpu.make_async_copy(
            w_hbm.at[tap, :, pl.ds(pl.multiple_of(n * CHUNK, CHUNK), CHUNK)], wbuf.at[n, tap], w_sem.at[n, tap]
        )

    low = rows // 4 - step
    high = rows - low

    def x_copy(start, stop, index):
        return pltpu.make_async_copy(
            x_hbm.at[pl.ds(start, stop - start)], xbuf.at[pl.ds(step + start, stop - start)], x_sem.at[index]
        )

    x_mid, x_low, x_high = x_copy(low, high, 0), x_copy(0, low, 1), x_copy(high, rows, 2)
    pos_copy = pltpu.make_async_copy(pos_hbm, pos_list.at[my_col], list_sem.at[0])
    bin_copy = pltpu.make_async_copy(bin_hbm, bin_list.at[my_col], list_sem.at[1])
    proj_copy = pltpu.make_async_copy(proj_hbm, proj_ref, end_sem.at[0])
    donor_copy = pltpu.make_async_copy(donor_hbm, donor_ref, end_sem.at[1])
    pos_copy.start()
    bin_copy.start()
    x_mid.start()
    for tap in range(3):
        w_copy(tap, 0).start()

    has_left = me > 0
    has_right = me < count - 1
    col_home = me // n_row
    self_col = col_home == my_col
    barrier = pltpu.get_barrier_semaphore()

    @pl.when(has_left)
    def _():
        pl.semaphore_signal(barrier, inc=1, device_id=place(me - 1), device_id_type=MESH)

    @pl.when(has_right)
    def _():
        pl.semaphore_signal(barrier, inc=1, device_id=place(me + 1), device_id_type=MESH)

    for d in range(1, n_col):
        pl.semaphore_signal(barrier, inc=1, device_id=(my_row, lax.rem(my_col + d, n_col)), device_id_type=MESH)
    for i in range(n_row):
        source = my_col * n_row + i

        @pl.when(source != me)
        def _():
            pl.semaphore_signal(barrier, inc=1, device_id=place(source), device_id_type=MESH)

    for tap in range(3):
        w_copy(tap, 1).start()
    x_low.start()
    x_high.start()
    for n in range(2, chunks):
        for tap in range(3):
            w_copy(tap, n).start()
    donor_copy.start()
    proj_copy.start()

    pos_copy.wait()
    bin_copy.wait()
    before = lax.broadcasted_iota(jnp.int32, (listed, listed), 0) < lax.broadcasted_iota(jnp.int32, (listed, listed), 1)
    before = hot(before).astype(BF16)
    kinds = max(16, n_col)
    kind = lax.broadcasted_iota(jnp.int32, (kinds, listed), 0)

    def group_of(acceptor):
        group = jnp.zeros_like(acceptor)
        for k in range(1, n_col):
            group = group + jnp.where(acceptor >= k * tile_cols, 1, 0)
        return group

    pos = pos_list[my_col]
    group = group_of(bin_list[my_col])
    in_group = hot(kind == group)
    rank = jnp.sum(in_group * dot(in_group.astype(BF16), before), axis=0, keepdims=True)
    slot = group.astype(F32) * float(CAP) + rank
    slot_hot = hot(lax.broadcasted_iota(jnp.int32, (slots, listed), 0).astype(F32) == slot).astype(BF16)
    pos_hot = hot(lax.broadcasted_iota(jnp.int32, (rows, listed), 0) == pos).astype(BF16)
    select[...] = dot_rows(slot_hot, pos_hot).astype(BF16)

    neighbours = jnp.where(has_left, 1, 0) + jnp.where(has_right, 1, 0)
    pl.semaphore_wait(barrier, neighbours + n_col - 1 + n_row - jnp.where(self_col, 1, 0))

    def up_copy():
        return pltpu.make_async_remote_copy(
            src_ref=x_hbm.at[pl.ds(0, step)],
            dst_ref=xbuf.at[pl.ds(rows + step, step)],
            send_sem=halo_send_sem.at[0],
            recv_sem=halo_recv_sem.at[0],
            device_id=place(me - 1),
            device_id_type=MESH,
        )

    def down_copy():
        return pltpu.make_async_remote_copy(
            src_ref=x_hbm.at[pl.ds(rows - step, step)],
            dst_ref=xbuf.at[pl.ds(0, step)],
            send_sem=halo_send_sem.at[1],
            recv_sem=halo_recv_sem.at[1],
            device_id=place(me + 1),
            device_id_type=MESH,
        )

    def row_group_copies(src, dst, send_sem, recv_sem, whole):
        copies = []
        for d in range(1, n_col):
            there = lax.rem(my_col + d, n_col)
            copies.append(
                pltpu.make_async_remote_copy(
                    src_ref=src if whole else src.at[there],
                    dst_ref=dst.at[my_col],
                    send_sem=send_sem.at[d - 1],
                    recv_sem=recv_sem.at[d - 1],
                    device_id=(my_row, there),
                    device_id_type=MESH,
                )
            )
        return copies

    def row_group_arrivals(src, dst, send_sem, recv_sem):
        for d in range(1, n_col):
            source = lax.rem(my_col + n_col - d, n_col)
            pltpu.make_async_remote_copy(
                src_ref=src,
                dst_ref=dst.at[source],
                send_sem=send_sem.at[d - 1],
                recv_sem=recv_sem.at[d - 1],
                device_id=(my_row, source),
                device_id_type=MESH,
            ).wait_recv()

    @pl.when(has_left)
    def _():
        up_copy().start()

    @pl.when(has_right)
    def _():
        down_copy().start()

    list_copies = row_group_copies(pos_hbm, pos_list, pos_send_sem, pos_recv_sem, True)
    list_copies += row_group_copies(bin_hbm, bin_list, bin_send_sem, bin_recv_sem, True)
    for copy in list_copies:
        copy.start()

    @pl.when(jnp.logical_not(has_left))
    def _():
        xbuf[0:step] = jnp.zeros((step, width), BF16)

    @pl.when(jnp.logical_not(has_right))
    def _():
        xbuf[rows + step : rows + 2 * step] = jnp.zeros((step, width), BF16)

    def combine(which, position, cols, ends):
        first = 2 * step * passes[which][position]

        def block(k):
            return xbuf[first + k * step : first + (k + 1) * step, cols]

        def put(k, value, scale):
            parts[which, k, position * step : (position + 1) * step, cols] = value * jnp.asarray(scale, BF16)

        group = passes[which][position]
        if (group == 0) == ends:
            put(0, block(0) - block(2), 0.5)
        if not ends:
            put(1, block(1) + block(2), 0.25)
            put(2, block(2) - block(1), 0.25)
        if (group == groups - 1) == ends:
            put(3, block(1) - block(3), 0.5)

    everything = slice(0, width)
    x_mid.wait()
    for position in range(len(passes[0])):
        combine(0, position, everything, False)

    def mix(n):
        outer = wbuf[n, 0] + wbuf[n, 2]
        inner = wbuf[n, 1]
        mixed[n, 0] = outer + inner
        mixed[n, 1] = outer - inner

    def products(which, n):
        cols = pl.ds(pl.multiple_of(n * CHUNK, CHUNK), CHUNK)
        plus = dot(parts[which, 1], mixed[n, 0])
        minus = dot(parts[which, 2], mixed[n, 1])
        even = (plus + minus) + dot(parts[which, 0], wbuf[n, 0])
        odd = (plus - minus) - dot(parts[which, 3], wbuf[n, 2])
        even = even + even * jnp.tanh(even)
        odd = odd + odd * jnp.tanh(odd)
        sums = []
        for position, group in enumerate(passes[which]):
            first = 2 * step * group
            mine = slice(position * step, (position + 1) * step)
            total = 0.0
            for k, value in enumerate((even[mine], odd[mine])):
                start = first + k * step
                out = xbuf[step + start : step + start + step, cols].astype(F32) + value
                hidden[start : start + step, cols] = out.astype(BF16)
                total = total + out
            sums.append(total)
        per_bin = POOL // (2 * step)
        for b in range(len(sums) // per_bin):
            which_bin = passes[which][b * per_bin] // per_bin
            total = sum(sums[b * per_bin + 1 : (b + 1) * per_bin], sums[b * per_bin])
            pooled[which_bin : which_bin + 1, cols] = jnp.sum(total, axis=0, keepdims=True) * (1.0 / POOL)

    def first_pass(n, carry):
        for tap in range(3):
            w_copy(tap, n).wait()
        mix(n)
        products(0, n)
        return carry

    lax.fori_loop(0, chunks, first_pass, 0)

    x_low.wait()
    x_high.wait()
    for position in range(len(passes[1])):
        combine(1, position, everything, False)

    donor_copy.wait()
    mid = slice(rows // 4, rows - rows // 4)
    donor_emb[mid] = dot(hidden[mid], donor_ref[...]).astype(BF16)

    @pl.when(has_left)
    def _():
        down_copy().wait_recv()

    @pl.when(has_right)
    def _():
        up_copy().wait_recv()

    for position in (0, len(passes[1]) - 1):
        combine(1, position, everything, True)

    def second_pass(n, carry):
        products(1, n)
        return carry

    lax.fori_loop(0, chunks, second_pass, 0)

    proj_copy.wait()
    means = pooled[...]
    scale = lax.rsqrt(jnp.mean(means * means, axis=-1, keepdims=True) + 1e-06)
    projected = dot((means * scale).astype(BF16), proj_ref[...]).astype(BF16).astype(F32)
    row_send[...] = projected[:, :LANES]
    col_send[...] = projected[:, LANES:]

    my_slot = me - col_home * n_row

    def col_copy(r):
        return pltpu.make_async_remote_copy(
            src_ref=col_send,
            dst_ref=cols_out.at[my_slot],
            send_sem=col_send_sem.at[r],
            recv_sem=col_recv_sem.at[my_slot],
            device_id=(r, col_home),
            device_id_type=MESH,
        )

    def is_other(r):
        return jnp.logical_or(jnp.logical_not(self_col), my_row != r)

    for r in range(n_row):

        @pl.when(is_other(r))
        def _():
            col_copy(r).start()

    row_copies = row_group_copies(row_send, rows_out, row_send_sem, row_recv_sem, True)
    for copy in row_copies:
        copy.start()

    for start in (0, rows - rows // 4):
        ends = slice(start, start + rows // 4)
        donor_emb[ends] = dot(hidden[ends], donor_ref[...]).astype(BF16)
    emb_send[...] = dot(select[...], donor_emb[...]).astype(BF16).reshape(n_col, CAP, LANES)
    emb_copies = row_group_copies(emb_send, emb_out, emb_send_sem, emb_recv_sem, False)
    for copy in emb_copies:
        copy.start()
    emb_out[my_col] = emb_send[my_col]
    rows_out[my_col] = row_send[...]

    @pl.when(self_col)
    def _():
        cols_out[my_slot] = col_send[...]

    row_group_arrivals(pos_hbm, pos_list, pos_send_sem, pos_recv_sem)
    row_group_arrivals(bin_hbm, bin_list, bin_send_sem, bin_recv_sem)
    col_lanes = coord_out.shape[2] - LANES
    mine = jnp.zeros((kinds, listed), F32)
    for k in range(n_col):
        mine = jnp.where((kind == k) & (group_of(bin_list[k]) == my_col), 1.0, mine)
    ranks = dot(mine.astype(BF16), before)
    ranks = jnp.where(mine > 0.0, ranks, -1.0)
    at = lax.broadcasted_iota(jnp.int32, (CAP, listed), 0).astype(F32)
    col_at = lax.broadcasted_iota(jnp.int32, (col_lanes, listed), 0)
    row_at = lax.broadcasted_iota(jnp.int32, (LANES, listed), 0) * POOL
    for k in range(n_col):
        here = hot(at == ranks[k : k + 1]).astype(BF16)
        pair_col = bin_list[k] - my_col * tile_cols
        where = pos_list[k]
        col_hot = hot(col_at == pair_col).astype(BF16)
        row_hot = hot((where >= row_at) & (where < row_at + POOL)).astype(BF16)
        coord_out[k] = dot_rows(here, jnp.concatenate([col_hot, row_hot], axis=0)).astype(BF16)

    row_group_arrivals(row_send, rows_out, row_send_sem, row_recv_sem)
    for i in range(n_row):
        source = my_col * n_row + i

        @pl.when(source != me)
        def _():
            pltpu.make_async_remote_copy(
                src_ref=col_send,
                dst_ref=cols_out.at[i],
                send_sem=col_send_sem.at[i],
                recv_sem=col_recv_sem.at[i],
                device_id=place(source),
                device_id_type=MESH,
            ).wait_recv()

    row_group_arrivals(emb_send.at[0], emb_out, emb_send_sem, emb_recv_sem)

    for copy in list_copies + row_copies + emb_copies:
        copy.wait_send()
    for r in range(n_row):

        @pl.when(is_other(r))
        def _():
            col_copy(r).wait_send()

    @pl.when(has_left)
    def _():
        up_copy().wait_send()

    @pl.when(has_right)
    def _():
        down_copy().wait_send()


def tiles(rows_ref, cols_ref, emb_ref, coord_ref, out_ref, pair_hbm, junction_ref, pair_ref, sem):
    n_col, bins, lanes = rows_ref.shape
    n_row = cols_ref.shape[0]
    tile_rows, tile_cols = n_col * bins, n_row * bins
    row_side = rows_ref[...].reshape(tile_rows, lanes)
    col_side = cols_ref[...].reshape(tile_cols, lanes)
    weight = out_ref[...]
    cap = emb_ref.shape[1]
    col_lanes = coord_ref.shape[2] - lanes
    side = min(8, tile_rows)
    copies = []
    for i in range(tile_rows // side):
        part = slice(i * side, (i + 1) * side)
        hidden = jnp.maximum(row_side[part, None, :] + col_side[None, :, :], 0.0).astype(BF16)
        pair_ref[part] = dot(hidden.reshape(side * tile_cols, lanes), weight).astype(BF16).reshape(side, tile_cols, lanes)
        copies.append(pltpu.make_async_copy(pair_ref.at[part], pair_hbm.at[part], sem.at[i]))
        copies[-1].start()
    coord = coord_ref[...]
    by_col = dot(coord[:, :, :tile_cols].reshape(n_col * cap, tile_cols), col_side.astype(BF16))
    by_row = [dot(coord[k, :, col_lanes : col_lanes + bins], rows_ref[k].astype(BF16)) for k in range(n_col)]
    hidden = jnp.maximum(jnp.concatenate(by_row, axis=0) + by_col, 0.0).astype(BF16)
    looked = dot(hidden, weight).astype(BF16)
    emb = emb_ref[...].reshape(n_col * cap, lanes)
    junction_ref[...] = jnp.maximum(emb.astype(F32) + looked.astype(F32), 0.0).astype(BF16)
    for copy in copies:
        copy.wait()


def local(n_row, n_col, sequence, filter_weight, pair_proj, pair_out, donor_w, donor_pos, acceptor_bin):
    rows, width = sequence.shape
    lanes = pair_out.shape[0]
    bins = rows // POOL
    listed = donor_pos.shape[0]
    chunks = width // CHUNK
    tile_rows, tile_cols = bins * n_col, bins * n_row
    col_lanes = -(-tile_cols // LANES) * LANES
    slots = n_col * CAP
    vmem = pl.BlockSpec(memory_space=pltpu.VMEM)
    hbm = pl.BlockSpec(memory_space=pl.ANY)
    dma = pltpu.SemaphoreType.DMA
    arrived = pl.pallas_call(
        functools.partial(trunk, n_row, n_col),
        out_shape=(
            pltpu.VMEM((n_col, bins, lanes), F32),
            pltpu.VMEM((n_row, bins, lanes), F32),
            pltpu.VMEM((n_col, CAP, lanes), BF16),
            pltpu.VMEM((n_col, CAP, col_lanes + LANES), BF16),
        ),
        in_specs=[hbm] * 6,
        out_specs=(vmem, vmem, vmem, vmem),
        scratch_shapes=[
            pltpu.VMEM((rows + 2 * DILATION_STEP, width), BF16),
            pltpu.VMEM((chunks, 3, width, CHUNK), BF16),
            pltpu.VMEM((chunks, 2, width, CHUNK), BF16),
            pltpu.VMEM((2, 4, rows // 4, width), BF16),
            pltpu.VMEM((rows, width), BF16),
            pltpu.VMEM((bins, width), F32),
            pltpu.VMEM((rows, lanes), BF16),
            pltpu.VMEM((slots, rows), BF16),
            pltpu.VMEM(pair_proj.shape, BF16),
            pltpu.VMEM(donor_w.shape, BF16),
            pltpu.VMEM((n_col, 1, listed), jnp.int32),
            pltpu.VMEM((n_col, 1, listed), jnp.int32),
            pltpu.VMEM((bins, lanes), F32),
            pltpu.VMEM((bins, lanes), F32),
            pltpu.VMEM((n_col, CAP, lanes), BF16),
            dma((3,)),
            dma((2,)),
            dma((chunks, 3)),
            dma((2,)),
            dma((2,)),
            dma((2,)),
            dma((n_col - 1,)),
            dma((n_col - 1,)),
            dma((n_col - 1,)),
            dma((n_col - 1,)),
            dma((n_col - 1,)),
            dma((n_col - 1,)),
            dma((n_col - 1,)),
            dma((n_col - 1,)),
            dma((n_row,)),
            dma((n_row,)),
        ],
        compiler_params=pltpu.CompilerParams(
            collective_id=0, has_side_effects=True, vmem_limit_bytes=56 * 1024 * 1024
        ),
        name="trunk",
    )(
        sequence,
        filter_weight,
        pair_proj,
        donor_w,
        donor_pos.reshape(1, listed),
        acceptor_bin.reshape(1, listed),
    )
    arrived = [pltpu.with_memory_space_constraint(a, pltpu.VMEM) for a in arrived]
    return pl.pallas_call(
        tiles,
        out_shape=(
            jax.ShapeDtypeStruct((tile_rows, tile_cols, lanes), BF16),
            jax.ShapeDtypeStruct((slots, lanes), BF16),
        ),
        in_specs=[vmem] * 5,
        out_specs=(hbm, vmem),
        scratch_shapes=[
            pltpu.VMEM((tile_rows, tile_cols, lanes), BF16),
            dma((tile_rows // min(8, tile_rows),)),
        ],
        name="tiles",
    )(*arrived, pair_out)


def solution(mesh):
    placed = (P(("row", "col"), None), P(), P(), P(), P(), P(("row", "col")), P(("row", "col")))
    return jax.shard_map(
        functools.partial(local, mesh.shape["row"], mesh.shape["col"]),
        mesh=mesh,
        in_specs=placed,
        out_specs=(P("row", "col", None), P(("row", "col"), None)),
        check_vma=False,
    )
```

```python
import functools

import jax
import jax.numpy as jnp
from jax import lax
from jax.experimental import pallas as pl
from jax.experimental.pallas import tpu as pltpu
from jax.sharding import PartitionSpec as P

DILATION_STEP = 32
POOL = 128
CAP = 64
LANES = 128
CHUNK = 512
AHEAD = 2
NEAR = 0.75
FAR = 1.5
MESH = pl.DeviceIdType.MESH
F32 = jnp.float32
BF16 = jnp.bfloat16


def dot(a, b):
    return jnp.dot(a, b, preferred_element_type=F32)


def dot_rows(a, b):
    return lax.dot_general(a, b, (((1,), (1,)), ((), ())), preferred_element_type=F32)


def hot(condition):
    return jnp.where(condition, 1.0, 0.0)


def trunk(
    n_row,
    n_col,
    x_hbm,
    w_hbm,
    proj_hbm,
    donor_hbm,
    out_hbm,
    pos_hbm,
    bin_hbm,
    rows_out,
    cols_out,
    emb_out,
    coord_out,
    weight_out,
    xbuf,
    wbuf,
    mixed,
    parts,
    kept,
    hidden,
    pooled,
    select,
    proj_ref,
    donor_ref,
    pos_list,
    bin_list,
    row_send,
    col_send,
    emb_send,
    x_sem,
    end_sem,
    w_sem,
    list_sem,
    halo_send_sem,
    halo_recv_sem,
    pos_send_sem,
    pos_recv_sem,
    bin_send_sem,
    bin_recv_sem,
    emb_send_sem,
    emb_recv_sem,
    row_send_sem,
    row_recv_sem,
    col_send_sem,
    col_recv_sem,
):
    rows, width = x_hbm.shape
    step = DILATION_STEP
    chunks = width // CHUNK
    bins = rows // POOL
    tile_cols = bins * n_row
    slots = n_col * CAP
    listed = pos_hbm.shape[1]
    count = n_row * n_col
    my_row = lax.axis_index("row")
    my_col = lax.axis_index("col")
    me = my_row * n_col + my_col

    groups = rows // POOL
    blocks = POOL // step

    def place(flat):
        return (flat // n_col, lax.rem(flat, n_col))

    def w_copy(tap, n):
        return pltpu.make_async_copy(
            w_hbm.at[tap, :, pl.ds(pl.multiple_of(n * CHUNK, CHUNK), CHUNK)], wbuf.at[n, tap], w_sem.at[n, tap]
        )

    half = rows // 2

    def x_copy(index):
        return pltpu.make_async_copy(
            x_hbm.at[pl.ds(index * half, half)], xbuf.at[pl.ds(step + index * half, half)], x_sem.at[index]
        )

    pos_copy = pltpu.make_async_copy(pos_hbm, pos_list.at[my_col], list_sem.at[0])
    bin_copy = pltpu.make_async_copy(bin_hbm, bin_list.at[my_col], list_sem.at[1])
    proj_copy = pltpu.make_async_copy(proj_hbm, proj_ref, end_sem.at[0])
    donor_copy = pltpu.make_async_copy(donor_hbm, donor_ref, end_sem.at[1])
    weight_copy = pltpu.make_async_copy(out_hbm, weight_out, end_sem.at[2])
    pos_copy.start()
    bin_copy.start()
    x_copy(0).start()
    x_copy(1).start()

    has_left = me > 0
    has_right = me < count - 1
    col_home = me // n_row
    self_col = col_home == my_col
    barrier = pltpu.get_barrier_semaphore()

    @pl.when(has_left)
    def _():
        pl.semaphore_signal(barrier, inc=1, device_id=place(me - 1), device_id_type=MESH)

    @pl.when(has_right)
    def _():
        pl.semaphore_signal(barrier, inc=1, device_id=place(me + 1), device_id_type=MESH)

    for d in range(1, n_col):
        pl.semaphore_signal(barrier, inc=1, device_id=(my_row, lax.rem(my_col + d, n_col)), device_id_type=MESH)
    for i in range(n_row):
        source = my_col * n_row + i

        @pl.when(source != me)
        def _():
            pl.semaphore_signal(barrier, inc=1, device_id=place(source), device_id_type=MESH)


    pos_copy.wait()
    bin_copy.wait()
    for tap in range(3):
        w_copy(tap, 0).start()
    before = lax.broadcasted_iota(jnp.int32, (listed, listed), 0) < lax.broadcasted_iota(jnp.int32, (listed, listed), 1)
    before = hot(before).astype(BF16)
    kinds = max(16, n_col)
    kind = lax.broadcasted_iota(jnp.int32, (kinds, listed), 0)

    def group_of(acceptor):
        group = jnp.zeros_like(acceptor)
        for k in range(1, n_col):
            group = group + jnp.where(acceptor >= k * tile_cols, 1, 0)
        return group

    pos = pos_list[my_col]
    group = group_of(bin_list[my_col])
    in_group = hot(kind == group)
    rank = jnp.sum(in_group * dot(in_group.astype(BF16), before), axis=0, keepdims=True)
    slot = group.astype(F32) * float(CAP) + rank
    slot_hot = hot(lax.broadcasted_iota(jnp.int32, (slots, listed), 0).astype(F32) == slot).astype(BF16)
    within = pos % POOL
    held = (within // step) * (groups * step) + (pos // POOL) * step + within % step
    pos_hot = hot(lax.broadcasted_iota(jnp.int32, (rows, listed), 0) == held).astype(BF16)
    select[...] = dot_rows(slot_hot, pos_hot).astype(BF16)

    def up_copy():
        return pltpu.make_async_remote_copy(
            src_ref=x_hbm.at[pl.ds(0, step)],
            dst_ref=xbuf.at[pl.ds(rows + step, step)],
            send_sem=halo_send_sem.at[0],
            recv_sem=halo_recv_sem.at[0],
            device_id=place(me - 1),
            device_id_type=MESH,
        )

    def down_copy():
        return pltpu.make_async_remote_copy(
            src_ref=x_hbm.at[pl.ds(rows - step, step)],
            dst_ref=xbuf.at[pl.ds(0, step)],
            send_sem=halo_send_sem.at[1],
            recv_sem=halo_recv_sem.at[1],
            device_id=place(me + 1),
            device_id_type=MESH,
        )

    def row_group_copies(src, dst, send_sem, recv_sem, whole):
        copies = []
        for d in range(1, n_col):
            there = lax.rem(my_col + d, n_col)
            copies.append(
                pltpu.make_async_remote_copy(
                    src_ref=src if whole else src.at[there],
                    dst_ref=dst.at[my_col],
                    send_sem=send_sem.at[d - 1],
                    recv_sem=recv_sem.at[d - 1],
                    device_id=(my_row, there),
                    device_id_type=MESH,
                )
            )
        return copies

    def row_group_arrivals(src, dst, send_sem, recv_sem):
        for d in range(1, n_col):
            source = lax.rem(my_col + n_col - d, n_col)
            pltpu.make_async_remote_copy(
                src_ref=src,
                dst_ref=dst.at[source],
                send_sem=send_sem.at[d - 1],
                recv_sem=recv_sem.at[d - 1],
                device_id=(my_row, source),
                device_id_type=MESH,
            ).wait_recv()

    @pl.when(jnp.logical_not(has_left))
    def _():
        xbuf[0:step] = jnp.zeros((step, width), BF16)

    @pl.when(jnp.logical_not(has_right))
    def _():
        xbuf[rows + step : rows + 2 * step] = jnp.zeros((step, width), BF16)

    near, far = NEAR * NEAR, FAR * FAR

    def block(group, k, cols):
        start = group * POOL + k * step
        return xbuf[start : start + step, cols].astype(F32)

    def put(k, group, cols, value):
        parts[k, group * step : (group + 1) * step, cols] = value.astype(BF16)

    def combine_inner(group, cols):
        one, two, three, four = (block(group, k, cols) for k in range(1, 5))
        by_near, by_far = 0.25 / (near * (near - far)), 0.25 / (far * (far - near))
        even = by_near * four - (by_near * far) * two
        odd = (NEAR * by_near) * three - (NEAR * by_near * far) * one
        put(1, group, cols, even + odd)
        put(2, group, cols, even - odd)
        even = by_far * four - (by_far * near) * two
        odd = (FAR * by_far) * three - (FAR * by_far * near) * one
        put(3, group, cols, even + odd)
        put(4, group, cols, even - odd)

    def combine_first(group, cols):
        zero, two, four = (block(group, k, cols) for k in (0, 2, 4))
        put(0, group, cols, 0.5 * zero - (0.5 * (near + far) / (near * far)) * two + (0.5 / (near * far)) * four)

    def combine_last(group, cols):
        one, three, five = (block(group, k, cols) for k in (1, 3, 5))
        put(5, group, cols, 0.5 * five - (0.5 * (near + far)) * three + (0.5 * near * far) * one)

    everything = slice(0, width)
    x_copy(0).wait()
    for group in range(groups // 2 - 1):
        combine_inner(group, everything)
    x_copy(1).wait()
    for n in range(1, AHEAD):
        for tap in range(3):
            w_copy(tap, n).start()
    for group in range(groups // 2 - 1, groups):
        combine_inner(group, everything)

    def mix(n):
        def scaled(value, by):
            return value * jnp.asarray(by, BF16)

        first, second, third = wbuf[n, 0], scaled(wbuf[n, 1], NEAR), scaled(wbuf[n, 2], near)
        outer = first + third
        mixed[0] = outer + second
        mixed[1] = outer - second
        outer = first + scaled(third, far / near)
        second = scaled(second, FAR / NEAR)
        mixed[2] = outer + second
        mixed[3] = outer - second

    def finish(k, value, cols):
        value = value + value * jnp.tanh(value)
        sums = []
        for group in range(groups):
            start = group * POOL + k * step
            out = xbuf[step + start : step + start + step, cols].astype(F32) + value[group * step : (group + 1) * step]
            sums.append(out)
            start = (k * groups + group) * step
            hidden[start : start + step, cols] = out.astype(BF16)
        return sums

    def pool(first, second):
        return jnp.concatenate([jnp.sum(a + b, axis=0, keepdims=True) for a, b in zip(first, second)], axis=0)

    def first_pass(n, carry):
        cols = pl.ds(pl.multiple_of(n * CHUNK, CHUNK), CHUNK)
        for tap in range(3):
            w_copy(tap, n).wait()

        @pl.when(n + AHEAD < chunks)
        def _():
            for tap in range(3):
                w_copy(tap, n + AHEAD).start()

        mix(n)
        plus, minus = dot(parts[1], mixed[0]), dot(parts[2], mixed[1])
        near_sum, near_gap = plus + minus, plus - minus
        plus, minus = dot(parts[3], mixed[2]), dot(parts[4], mixed[3])
        far_sum, far_gap = plus + minus, plus - minus
        kept[0, :, cols] = near_sum + far_sum
        kept[1, :, cols] = (NEAR * near) * near_gap + (FAR * far) * far_gap
        second = finish(1, NEAR * near_gap + FAR * far_gap, cols)
        third = finish(2, near * near_sum + far * far_sum, cols)
        pooled[:, cols] = pool(second, third)
        for group in range(groups):
            if group > 0:
                combine_first(group, cols)
            if group < groups - 1:
                combine_last(group, cols)
        return carry

    neighbours = jnp.where(has_left, 1, 0) + jnp.where(has_right, 1, 0)
    pl.semaphore_wait(barrier, neighbours + n_col - 1 + n_row - jnp.where(self_col, 1, 0))

    @pl.when(has_left)
    def _():
        up_copy().start()

    @pl.when(has_right)
    def _():
        down_copy().start()

    list_copies = row_group_copies(pos_hbm, pos_list, pos_send_sem, pos_recv_sem, True)
    list_copies += row_group_copies(bin_hbm, bin_list, bin_send_sem, bin_recv_sem, True)
    for copy in list_copies:
        copy.start()

    donor_copy.start()
    proj_copy.start()
    weight_copy.start()
    lax.fori_loop(0, chunks, first_pass, 0)

    @pl.when(has_left)
    def _():
        down_copy().wait_recv()

    @pl.when(has_right)
    def _():
        up_copy().wait_recv()

    combine_first(0, everything)
    combine_last(groups - 1, everything)

    donor_copy.wait()
    proj_copy.wait()
    weight_copy.wait()
    quarter = rows // blocks
    inner = slice(quarter, rows - quarter)

    def donor(held, n):
        cols = slice(n * CHUNK, (n + 1) * CHUNK)
        return dot(hidden[held, cols], donor_ref[cols])

    emb_inner = emb_first = emb_last = projected = square = 0.0
    for n in range(chunks):
        cols = slice(n * CHUNK, (n + 1) * CHUNK)
        first = finish(0, kept[0, :, cols] + dot(parts[0], wbuf[n, 0]), cols)
        fourth = finish(blocks - 1, kept[1, :, cols] + dot(parts[5], wbuf[n, 2]), cols)
        emb_inner += donor(inner, n)
        means = (pooled[:, cols] + pool(first, fourth)) * (1.0 / POOL)
        square += jnp.sum(means * means, axis=-1, keepdims=True)
        projected += dot(means.astype(BF16), proj_ref[cols])
        if n < chunks - 1:
            emb_first += donor(slice(0, quarter), n)
            emb_last += donor(slice(rows - quarter, rows), n)
    projected = (projected * lax.rsqrt(square * (1.0 / width) + 1e-06)).astype(BF16).astype(F32)
    row_send[...] = projected[:, :LANES]
    col_send[...] = projected[:, LANES:]

    my_slot = me - col_home * n_row

    def col_copy(r):
        return pltpu.make_async_remote_copy(
            src_ref=col_send,
            dst_ref=cols_out.at[my_slot],
            send_sem=col_send_sem.at[r],
            recv_sem=col_recv_sem.at[my_slot],
            device_id=(r, col_home),
            device_id_type=MESH,
        )

    def is_other(r):
        return jnp.logical_or(jnp.logical_not(self_col), my_row != r)

    for r in range(n_row):

        @pl.when(is_other(r))
        def _():
            col_copy(r).start()

    row_copies = row_group_copies(row_send, rows_out, row_send_sem, row_recv_sem, True)
    for copy in row_copies:
        copy.start()

    emb_first += donor(slice(0, quarter), chunks - 1)
    emb_last += donor(slice(rows - quarter, rows), chunks - 1)
    donor_emb = jnp.concatenate([emb_first, emb_inner, emb_last], axis=0).astype(BF16)
    emb_send[...] = dot(select[...], donor_emb).astype(BF16).reshape(n_col, CAP, LANES)
    emb_copies = row_group_copies(emb_send, emb_out, emb_send_sem, emb_recv_sem, False)
    for copy in emb_copies:
        copy.start()
    emb_out[my_col] = emb_send[my_col]
    rows_out[my_col] = row_send[...]

    @pl.when(self_col)
    def _():
        cols_out[my_slot] = col_send[...]

    row_group_arrivals(pos_hbm, pos_list, pos_send_sem, pos_recv_sem)
    row_group_arrivals(bin_hbm, bin_list, bin_send_sem, bin_recv_sem)
    col_lanes = coord_out.shape[2] - LANES
    mine = jnp.zeros((kinds, listed), F32)
    for k in range(n_col):
        mine = jnp.where((kind == k) & (group_of(bin_list[k]) == my_col), 1.0, mine)
    ranks = dot(mine.astype(BF16), before)
    ranks = jnp.where(mine > 0.0, ranks, -1.0)
    at = lax.broadcasted_iota(jnp.int32, (CAP, listed), 0).astype(F32)
    col_at = lax.broadcasted_iota(jnp.int32, (col_lanes, listed), 0)
    row_at = lax.broadcasted_iota(jnp.int32, (LANES, listed), 0) * POOL
    for k in range(n_col):
        here = hot(at == ranks[k : k + 1]).astype(BF16)
        pair_col = bin_list[k] - my_col * tile_cols
        where = pos_list[k]
        col_hot = hot(col_at == pair_col).astype(BF16)
        row_hot = hot((where >= row_at) & (where < row_at + POOL)).astype(BF16)
        coord_out[k] = dot_rows(here, jnp.concatenate([col_hot, row_hot], axis=0)).astype(BF16)

    row_group_arrivals(row_send, rows_out, row_send_sem, row_recv_sem)
    for i in range(n_row):
        source = my_col * n_row + i

        @pl.when(source != me)
        def _():
            pltpu.make_async_remote_copy(
                src_ref=col_send,
                dst_ref=cols_out.at[i],
                send_sem=col_send_sem.at[i],
                recv_sem=col_recv_sem.at[i],
                device_id=place(source),
                device_id_type=MESH,
            ).wait_recv()

    row_group_arrivals(emb_send.at[0], emb_out, emb_send_sem, emb_recv_sem)

    for copy in list_copies + row_copies + emb_copies:
        copy.wait_send()
    for r in range(n_row):

        @pl.when(is_other(r))
        def _():
            col_copy(r).wait_send()

    @pl.when(has_left)
    def _():
        up_copy().wait_send()

    @pl.when(has_right)
    def _():
        down_copy().wait_send()


def tiles(rows_ref, cols_ref, emb_ref, coord_ref, out_ref, pair_hbm, junction_hbm, pair_ref, junction_ref, sem):
    n_col, bins, lanes = rows_ref.shape
    n_row = cols_ref.shape[0]
    tile_rows, tile_cols = n_col * bins, n_row * bins
    row_side = rows_ref[...].reshape(tile_rows, lanes)
    col_side = cols_ref[...].reshape(tile_cols, lanes)
    weight = out_ref[...]
    cap = emb_ref.shape[1]
    col_lanes = coord_ref.shape[2] - lanes
    side = min(8, tile_rows)
    copies = []
    for i in range(tile_rows // side):
        part = slice(i * side, (i + 1) * side)
        hidden = jnp.maximum(row_side[part, None, :] + col_side[None, :, :], 0.0).astype(BF16)
        pair_ref[part] = dot(hidden.reshape(side * tile_cols, lanes), weight).astype(BF16).reshape(side, tile_cols, lanes)
        copies.append(pltpu.make_async_copy(pair_ref.at[part], pair_hbm.at[part], sem.at[i]))
        copies[-1].start()
    coord = coord_ref[...]
    by_col = dot(coord[:, :, :tile_cols].reshape(n_col * cap, tile_cols), col_side.astype(BF16))
    by_row = [dot(coord[k, :, col_lanes : col_lanes + bins], rows_ref[k].astype(BF16)) for k in range(n_col)]
    hidden = jnp.maximum(jnp.concatenate(by_row, axis=0) + by_col, 0.0).astype(BF16)
    looked = dot(hidden, weight).astype(BF16)
    emb = emb_ref[...].reshape(n_col * cap, lanes)
    junction_ref[...] = jnp.maximum(emb.astype(F32) + looked.astype(F32), 0.0).astype(BF16)
    copies.append(pltpu.make_async_copy(junction_ref, junction_hbm, sem.at[len(copies)]))
    copies[-1].start()
    for copy in copies:
        copy.wait()


def local(n_row, n_col, sequence, filter_weight, pair_proj, pair_out, donor_w, donor_pos, acceptor_bin):
    rows, width = sequence.shape
    lanes = pair_out.shape[0]
    bins = rows // POOL
    listed = donor_pos.shape[0]
    chunks = width // CHUNK
    tile_rows, tile_cols = bins * n_col, bins * n_row
    col_lanes = -(-tile_cols // LANES) * LANES
    slots = n_col * CAP
    vmem = pl.BlockSpec(memory_space=pltpu.VMEM)
    hbm = pl.BlockSpec(memory_space=pl.ANY)
    dma = pltpu.SemaphoreType.DMA
    arrived = pl.pallas_call(
        functools.partial(trunk, n_row, n_col),
        out_shape=(
            pltpu.VMEM((n_col, bins, lanes), F32),
            pltpu.VMEM((n_row, bins, lanes), F32),
            pltpu.VMEM((n_col, CAP, lanes), BF16),
            pltpu.VMEM((n_col, CAP, col_lanes + LANES), BF16),
            pltpu.VMEM(pair_out.shape, BF16),
        ),
        in_specs=[hbm] * 7,
        out_specs=(vmem,) * 5,
        scratch_shapes=[
            pltpu.VMEM((rows + 2 * DILATION_STEP, width), BF16),
            pltpu.VMEM((chunks, 3, width, CHUNK), BF16),
            pltpu.VMEM((4, width, CHUNK), BF16),
            pltpu.VMEM((6, rows // 4, width), BF16),
            pltpu.VMEM((2, rows // 4, width), F32),
            pltpu.VMEM((rows, width), BF16),
            pltpu.VMEM((bins, width), F32),
            pltpu.VMEM((slots, rows), BF16),
            pltpu.VMEM(pair_proj.shape, BF16),
            pltpu.VMEM(donor_w.shape, BF16),
            pltpu.VMEM((n_col, 1, listed), jnp.int32),
            pltpu.VMEM((n_col, 1, listed), jnp.int32),
            pltpu.VMEM((bins, lanes), F32),
            pltpu.VMEM((bins, lanes), F32),
            pltpu.VMEM((n_col, CAP, lanes), BF16),
            dma((2,)),
            dma((3,)),
            dma((chunks, 3)),
            dma((2,)),
            dma((2,)),
            dma((2,)),
            dma((n_col - 1,)),
            dma((n_col - 1,)),
            dma((n_col - 1,)),
            dma((n_col - 1,)),
            dma((n_col - 1,)),
            dma((n_col - 1,)),
            dma((n_col - 1,)),
            dma((n_col - 1,)),
            dma((n_row,)),
            dma((n_row,)),
        ],
        compiler_params=pltpu.CompilerParams(
            collective_id=0, has_side_effects=True, vmem_limit_bytes=56 * 1024 * 1024
        ),
        name="trunk",
    )(
        sequence,
        filter_weight,
        pair_proj,
        donor_w,
        pair_out,
        donor_pos.reshape(1, listed),
        acceptor_bin.reshape(1, listed),
    )
    arrived = [pltpu.with_memory_space_constraint(a, pltpu.VMEM) for a in arrived]
    return pl.pallas_call(
        tiles,
        out_shape=(
            jax.ShapeDtypeStruct((tile_rows, tile_cols, lanes), BF16),
            jax.ShapeDtypeStruct((slots, lanes), BF16),
        ),
        in_specs=[vmem] * 5,
        out_specs=(hbm, hbm),
        scratch_shapes=[
            pltpu.VMEM((tile_rows, tile_cols, lanes), BF16),
            pltpu.VMEM((slots, lanes), BF16),
            dma((tile_rows // min(8, tile_rows) + 1,)),
        ],
        name="tiles",
    )(*arrived)


def solution(mesh):
    placed = (P(("row", "col"), None), P(), P(), P(), P(), P(("row", "col")), P(("row", "col")))
    return jax.shard_map(
        functools.partial(local, mesh.shape["row"], mesh.shape["col"]),
        mesh=mesh,
        in_specs=placed,
        out_specs=(P("row", "col", None), P(("row", "col"), None)),
        check_vma=False,
    )
```

```python
import functools

import jax
import jax.numpy as jnp
from jax import lax
from jax.experimental import pallas as pl
from jax.experimental.pallas import tpu as pltpu
from jax.sharding import PartitionSpec as P

DILATION_STEP = 32
POOL = 128
CAP = 64
LANES = 128
CHUNK = 256
AHEAD = 3
NEAR = 0.75
FAR = 1.5
MESH = pl.DeviceIdType.MESH
F32 = jnp.float32
BF16 = jnp.bfloat16


def dot(a, b):
    return jnp.dot(a, b, preferred_element_type=F32)


def dot_rows(a, b):
    return lax.dot_general(a, b, (((1,), (1,)), ((), ())), preferred_element_type=F32)


def hot(condition):
    return jnp.where(condition, 1.0, 0.0)


def trunk(
    n_row,
    n_col,
    x_hbm,
    w_hbm,
    proj_hbm,
    donor_hbm,
    out_hbm,
    pos_hbm,
    bin_hbm,
    pair_out,
    junction_out,
    rows_out,
    cols_out,
    emb_out,
    weight_out,
    xbuf,
    wbuf,
    mixed,
    parts,
    kept,
    hidden,
    pooled,
    select,
    proj_ref,
    donor_ref,
    pos_list,
    bin_list,
    row_send,
    col_send,
    emb_send,
    x_sem,
    end_sem,
    w_sem,
    list_sem,
    halo_send_sem,
    halo_recv_sem,
    pos_send_sem,
    pos_recv_sem,
    bin_send_sem,
    bin_recv_sem,
    emb_send_sem,
    emb_recv_sem,
    row_send_sem,
    row_recv_sem,
    col_send_sem,
    col_recv_sem,
):
    rows, width = x_hbm.shape
    step = DILATION_STEP
    chunks = width // CHUNK
    bins = rows // POOL
    tile_cols = bins * n_row
    slots = n_col * CAP
    listed = pos_hbm.shape[1]
    count = n_row * n_col
    my_row = lax.axis_index("row")
    my_col = lax.axis_index("col")
    me = my_row * n_col + my_col

    groups = rows // POOL
    blocks = POOL // step

    def place(flat):
        return (flat // n_col, lax.rem(flat, n_col))

    def w_copy(tap, n):
        return pltpu.make_async_copy(
            w_hbm.at[tap, :, pl.ds(pl.multiple_of(n * CHUNK, CHUNK), CHUNK)], wbuf.at[n, tap], w_sem.at[n, tap]
        )

    half = rows // 2

    def x_copy(index):
        return pltpu.make_async_copy(
            x_hbm.at[pl.ds(index * half, half)], xbuf.at[pl.ds(step + index * half, half)], x_sem.at[index]
        )

    pos_copy = pltpu.make_async_copy(pos_hbm, pos_list.at[my_col], list_sem.at[0])
    bin_copy = pltpu.make_async_copy(bin_hbm, bin_list.at[my_col], list_sem.at[1])
    proj_copy = pltpu.make_async_copy(proj_hbm, proj_ref, end_sem.at[0])
    donor_copy = pltpu.make_async_copy(donor_hbm, donor_ref, end_sem.at[1])
    weight_copy = pltpu.make_async_copy(out_hbm, weight_out, end_sem.at[2])
    pos_copy.start()
    bin_copy.start()
    x_copy(0).start()
    x_copy(1).start()

    has_left = me > 0
    has_right = me < count - 1
    col_home = me // n_row
    self_col = col_home == my_col
    barrier = pltpu.get_barrier_semaphore()

    @pl.when(has_left)
    def _():
        pl.semaphore_signal(barrier, inc=1, device_id=place(me - 1), device_id_type=MESH)

    @pl.when(has_right)
    def _():
        pl.semaphore_signal(barrier, inc=1, device_id=place(me + 1), device_id_type=MESH)

    for d in range(1, n_col):
        pl.semaphore_signal(barrier, inc=1, device_id=(my_row, lax.rem(my_col + d, n_col)), device_id_type=MESH)
    for i in range(n_row):
        source = my_col * n_row + i

        @pl.when(source != me)
        def _():
            pl.semaphore_signal(barrier, inc=1, device_id=place(source), device_id_type=MESH)


    pos_copy.wait()
    bin_copy.wait()
    for tap in range(3):
        w_copy(tap, 0).start()
    before = lax.broadcasted_iota(jnp.int32, (listed, listed), 0) < lax.broadcasted_iota(jnp.int32, (listed, listed), 1)
    before = hot(before).astype(BF16)
    kinds = max(16, n_col)
    kind = lax.broadcasted_iota(jnp.int32, (kinds, listed), 0)

    def group_of(acceptor):
        group = jnp.zeros_like(acceptor)
        for k in range(1, n_col):
            group = group + jnp.where(acceptor >= k * tile_cols, 1, 0)
        return group

    pos = pos_list[my_col]
    group = group_of(bin_list[my_col])
    in_group = hot(kind == group)
    rank = jnp.sum(in_group * dot(in_group.astype(BF16), before), axis=0, keepdims=True)
    slot = group.astype(F32) * float(CAP) + rank
    slot_hot = hot(lax.broadcasted_iota(jnp.int32, (slots, listed), 0).astype(F32) == slot).astype(BF16)
    within = pos % POOL
    held = (within // step) * (groups * step) + (pos // POOL) * step + within % step
    pos_hot = hot(lax.broadcasted_iota(jnp.int32, (rows, listed), 0) == held).astype(BF16)
    select[...] = dot_rows(slot_hot, pos_hot).astype(BF16)

    def up_copy():
        return pltpu.make_async_remote_copy(
            src_ref=x_hbm.at[pl.ds(0, step)],
            dst_ref=xbuf.at[pl.ds(rows + step, step)],
            send_sem=halo_send_sem.at[0],
            recv_sem=halo_recv_sem.at[0],
            device_id=place(me - 1),
            device_id_type=MESH,
        )

    def down_copy():
        return pltpu.make_async_remote_copy(
            src_ref=x_hbm.at[pl.ds(rows - step, step)],
            dst_ref=xbuf.at[pl.ds(0, step)],
            send_sem=halo_send_sem.at[1],
            recv_sem=halo_recv_sem.at[1],
            device_id=place(me + 1),
            device_id_type=MESH,
        )

    def row_group_copies(src, dst, send_sem, recv_sem, whole):
        copies = []
        for d in range(1, n_col):
            there = lax.rem(my_col + d, n_col)
            copies.append(
                pltpu.make_async_remote_copy(
                    src_ref=src if whole else src.at[there],
                    dst_ref=dst.at[my_col],
                    send_sem=send_sem.at[d - 1],
                    recv_sem=recv_sem.at[d - 1],
                    device_id=(my_row, there),
                    device_id_type=MESH,
                )
            )
        return copies

    def row_group_arrivals(src, dst, send_sem, recv_sem):
        for d in range(1, n_col):
            source = lax.rem(my_col + n_col - d, n_col)
            pltpu.make_async_remote_copy(
                src_ref=src,
                dst_ref=dst.at[source],
                send_sem=send_sem.at[d - 1],
                recv_sem=recv_sem.at[d - 1],
                device_id=(my_row, source),
                device_id_type=MESH,
            ).wait_recv()

    @pl.when(jnp.logical_not(has_left))
    def _():
        xbuf[0:step] = jnp.zeros((step, width), BF16)

    @pl.when(jnp.logical_not(has_right))
    def _():
        xbuf[rows + step : rows + 2 * step] = jnp.zeros((step, width), BF16)

    near, far = NEAR * NEAR, FAR * FAR

    def block(group, k, cols):
        start = group * POOL + k * step
        return xbuf[start : start + step, cols].astype(F32)

    def put(k, group, cols, value):
        parts[k, group * step : (group + 1) * step, cols] = value.astype(BF16)

    def combine_inner(group, cols):
        one, two, three, four = (block(group, k, cols) for k in range(1, 5))
        by_near, by_far = 0.25 / (near * (near - far)), 0.25 / (far * (far - near))
        even = by_near * four - (by_near * far) * two
        odd = (NEAR * by_near) * three - (NEAR * by_near * far) * one
        put(1, group, cols, even + odd)
        put(2, group, cols, even - odd)
        even = by_far * four - (by_far * near) * two
        odd = (FAR * by_far) * three - (FAR * by_far * near) * one
        put(3, group, cols, even + odd)
        put(4, group, cols, even - odd)

    def combine_first(group, cols):
        zero, two, four = (block(group, k, cols) for k in (0, 2, 4))
        put(0, group, cols, 0.5 * zero - (0.5 * (near + far) / (near * far)) * two + (0.5 / (near * far)) * four)

    def combine_last(group, cols):
        one, three, five = (block(group, k, cols) for k in (1, 3, 5))
        put(5, group, cols, 0.5 * five - (0.5 * (near + far)) * three + (0.5 * near * far) * one)

    everything = slice(0, width)
    x_copy(0).wait()
    for group in range(groups // 2 - 1):
        combine_inner(group, everything)
    x_copy(1).wait()
    for n in range(1, AHEAD):
        for tap in range(3):
            w_copy(tap, n).start()
    for group in range(groups // 2 - 1, groups):
        combine_inner(group, everything)

    def mix(n):
        def scaled(value, by):
            return value * jnp.asarray(by, BF16)

        first, second, third = wbuf[n, 0], scaled(wbuf[n, 1], NEAR), scaled(wbuf[n, 2], near)
        outer = first + third
        mixed[0] = outer + second
        mixed[1] = outer - second
        outer = first + scaled(third, far / near)
        second = scaled(second, FAR / NEAR)
        mixed[2] = outer + second
        mixed[3] = outer - second

    def finish(k, value, cols):
        value = value + value * jnp.tanh(value)
        sums = []
        for group in range(groups):
            start = group * POOL + k * step
            out = xbuf[step + start : step + start + step, cols].astype(F32) + value[group * step : (group + 1) * step]
            sums.append(out)
            start = (k * groups + group) * step
            hidden[start : start + step, cols] = out.astype(BF16)
        return sums

    def pool(first, second):
        return jnp.concatenate([jnp.sum(a + b, axis=0, keepdims=True) for a, b in zip(first, second)], axis=0)

    def first_pass(n, carry):
        cols = pl.ds(pl.multiple_of(n * CHUNK, CHUNK), CHUNK)
        for tap in range(3):
            w_copy(tap, n).wait()

        @pl.when(n + AHEAD < chunks)
        def _():
            for tap in range(3):
                w_copy(tap, n + AHEAD).start()

        mix(n)
        plus, minus = dot(parts[1], mixed[0]), dot(parts[2], mixed[1])
        near_sum, near_gap = plus + minus, plus - minus
        plus, minus = dot(parts[3], mixed[2]), dot(parts[4], mixed[3])
        far_sum, far_gap = plus + minus, plus - minus
        kept[0, :, cols] = near_sum + far_sum
        kept[1, :, cols] = (NEAR * near) * near_gap + (FAR * far) * far_gap
        second = finish(1, NEAR * near_gap + FAR * far_gap, cols)
        third = finish(2, near * near_sum + far * far_sum, cols)
        pooled[:, cols] = pool(second, third)
        for group in range(groups):
            if group > 0:
                combine_first(group, cols)
            if group < groups - 1:
                combine_last(group, cols)
        return carry

    neighbours = jnp.where(has_left, 1, 0) + jnp.where(has_right, 1, 0)
    pl.semaphore_wait(barrier, neighbours + n_col - 1 + n_row - jnp.where(self_col, 1, 0))

    @pl.when(has_left)
    def _():
        up_copy().start()

    @pl.when(has_right)
    def _():
        down_copy().start()

    list_copies = row_group_copies(pos_hbm, pos_list, pos_send_sem, pos_recv_sem, True)
    list_copies += row_group_copies(bin_hbm, bin_list, bin_send_sem, bin_recv_sem, True)
    for copy in list_copies:
        copy.start()

    donor_copy.start()
    proj_copy.start()
    weight_copy.start()
    lax.fori_loop(0, chunks, first_pass, 0)

    @pl.when(has_left)
    def _():
        down_copy().wait_recv()

    @pl.when(has_right)
    def _():
        up_copy().wait_recv()

    combine_first(0, everything)
    combine_last(groups - 1, everything)

    donor_copy.wait()
    proj_copy.wait()
    weight_copy.wait()
    quarter = rows // blocks
    inner = slice(quarter, rows - quarter)

    def donor(held, n):
        cols = slice(n * CHUNK, (n + 1) * CHUNK)
        return dot(hidden[held, cols], donor_ref[cols])

    emb_inner = emb_first = emb_last = projected = square = 0.0
    for n in range(chunks):
        cols = slice(n * CHUNK, (n + 1) * CHUNK)
        first = finish(0, kept[0, :, cols] + dot(parts[0], wbuf[n, 0]), cols)
        fourth = finish(blocks - 1, kept[1, :, cols] + dot(parts[5], wbuf[n, 2]), cols)
        emb_inner += donor(inner, n)
        means = (pooled[:, cols] + pool(first, fourth)) * (1.0 / POOL)
        square += jnp.sum(means * means, axis=-1, keepdims=True)
        projected += dot(means.astype(BF16), proj_ref[cols])
        if n < chunks - 1:
            emb_first += donor(slice(0, quarter), n)
            emb_last += donor(slice(rows - quarter, rows), n)
    projected = (projected * lax.rsqrt(square * (1.0 / width) + 1e-06)).astype(BF16).astype(F32)
    row_send[...] = projected[:, :LANES]
    col_send[...] = projected[:, LANES:]

    my_slot = me - col_home * n_row

    def col_copy(r):
        return pltpu.make_async_remote_copy(
            src_ref=col_send,
            dst_ref=cols_out.at[my_slot],
            send_sem=col_send_sem.at[r],
            recv_sem=col_recv_sem.at[my_slot],
            device_id=(r, col_home),
            device_id_type=MESH,
        )

    def is_other(r):
        return jnp.logical_or(jnp.logical_not(self_col), my_row != r)

    for r in range(n_row):

        @pl.when(is_other(r))
        def _():
            col_copy(r).start()

    row_copies = row_group_copies(row_send, rows_out, row_send_sem, row_recv_sem, True)
    for copy in row_copies:
        copy.start()

    emb_first += donor(slice(0, quarter), chunks - 1)
    emb_last += donor(slice(rows - quarter, rows), chunks - 1)
    donor_emb = jnp.concatenate([emb_first, emb_inner, emb_last], axis=0).astype(BF16)
    emb_send[...] = dot(select[...], donor_emb).astype(BF16).reshape(n_col, CAP, LANES)
    emb_copies = row_group_copies(emb_send, emb_out, emb_send_sem, emb_recv_sem, False)
    for copy in emb_copies:
        copy.start()
    emb_out[my_col] = emb_send[my_col]
    rows_out[my_col] = row_send[...]

    @pl.when(self_col)
    def _():
        cols_out[my_slot] = col_send[...]

    row_group_arrivals(pos_hbm, pos_list, pos_send_sem, pos_recv_sem)
    row_group_arrivals(bin_hbm, bin_list, bin_send_sem, bin_recv_sem)
    col_lanes = -(-tile_cols // LANES) * LANES
    mine = jnp.zeros((kinds, listed), F32)
    for k in range(n_col):
        mine = jnp.where((kind == k) & (group_of(bin_list[k]) == my_col), 1.0, mine)
    ranks = dot(mine.astype(BF16), before)
    ranks = jnp.where(mine > 0.0, ranks, -1.0)
    at = lax.broadcasted_iota(jnp.int32, (CAP, listed), 0).astype(F32)
    col_at = lax.broadcasted_iota(jnp.int32, (col_lanes, listed), 0)
    row_at = lax.broadcasted_iota(jnp.int32, (LANES, listed), 0) * POOL
    col_coords, row_coords = [], []
    for k in range(n_col):
        here = hot(at == ranks[k : k + 1]).astype(BF16)
        pair_col = bin_list[k] - my_col * tile_cols
        where = pos_list[k]
        col_hot = hot(col_at == pair_col).astype(BF16)
        row_hot = hot((where >= row_at) & (where < row_at + POOL)).astype(BF16)
        coord = dot_rows(here, jnp.concatenate([col_hot, row_hot], axis=0)).astype(BF16)
        col_coords.append(coord[:, :tile_cols])
        row_coords.append(coord[:, col_lanes : col_lanes + bins])

    row_group_arrivals(row_send, rows_out, row_send_sem, row_recv_sem)
    for i in range(n_row):
        source = my_col * n_row + i

        @pl.when(source != me)
        def _():
            pltpu.make_async_remote_copy(
                src_ref=col_send,
                dst_ref=cols_out.at[i],
                send_sem=col_send_sem.at[i],
                recv_sem=col_recv_sem.at[i],
                device_id=place(source),
                device_id_type=MESH,
            ).wait_recv()

    tile_rows = bins * n_col
    weight = weight_out[...]
    row_side = rows_out[...].reshape(tile_rows, LANES)
    col_side = cols_out[...].reshape(tile_cols, LANES)
    side = min(8, tile_rows)
    for i in range(tile_rows // side):
        part = slice(i * side, (i + 1) * side)
        sums = jnp.maximum(row_side[part, None, :] + col_side[None, :, :], 0.0).astype(BF16)
        pair_out[part] = dot(sums.reshape(side * tile_cols, LANES), weight).astype(BF16).reshape(side, tile_cols, LANES)
    by_col = dot(jnp.concatenate(col_coords, axis=0), col_side.astype(BF16))
    by_row = [dot(row_coords[k], rows_out[k].astype(BF16)) for k in range(n_col)]
    sums = jnp.maximum(jnp.concatenate(by_row, axis=0) + by_col, 0.0).astype(BF16)
    looked = dot(sums, weight).astype(BF16).astype(F32)

    row_group_arrivals(emb_send.at[0], emb_out, emb_send_sem, emb_recv_sem)
    junction_out[...] = jnp.maximum(emb_out[...].reshape(slots, LANES).astype(F32) + looked, 0.0).astype(BF16)

    for copy in list_copies + row_copies + emb_copies:
        copy.wait_send()
    for r in range(n_row):

        @pl.when(is_other(r))
        def _():
            col_copy(r).wait_send()

    @pl.when(has_left)
    def _():
        up_copy().wait_send()

    @pl.when(has_right)
    def _():
        down_copy().wait_send()


def leave(pair_ref, junction_ref, pair_hbm, junction_hbm, sem):
    copies = [
        pltpu.make_async_copy(pair_ref, pair_hbm, sem.at[0]),
        pltpu.make_async_copy(junction_ref, junction_hbm, sem.at[1]),
    ]
    for copy in copies:
        copy.start()
    for copy in copies:
        copy.wait()


def local(n_row, n_col, sequence, filter_weight, pair_proj, pair_out, donor_w, donor_pos, acceptor_bin):
    rows, width = sequence.shape
    lanes = pair_out.shape[0]
    bins = rows // POOL
    listed = donor_pos.shape[0]
    chunks = width // CHUNK
    tile_rows, tile_cols = bins * n_col, bins * n_row
    slots = n_col * CAP
    vmem = pl.BlockSpec(memory_space=pltpu.VMEM)
    hbm = pl.BlockSpec(memory_space=pl.ANY)
    dma = pltpu.SemaphoreType.DMA
    done = pl.pallas_call(
        functools.partial(trunk, n_row, n_col),
        out_shape=(
            pltpu.VMEM((tile_rows, tile_cols, lanes), BF16),
            pltpu.VMEM((slots, lanes), BF16),
        ),
        in_specs=[hbm] * 7,
        out_specs=(vmem, vmem),
        scratch_shapes=[
            pltpu.VMEM((n_col, bins, lanes), F32),
            pltpu.VMEM((n_row, bins, lanes), F32),
            pltpu.VMEM((n_col, CAP, lanes), BF16),
            pltpu.VMEM(pair_out.shape, BF16),
            pltpu.VMEM((rows + 2 * DILATION_STEP, width), BF16),
            pltpu.VMEM((chunks, 3, width, CHUNK), BF16),
            pltpu.VMEM((4, width, CHUNK), BF16),
            pltpu.VMEM((6, rows // 4, width), BF16),
            pltpu.VMEM((2, rows // 4, width), F32),
            pltpu.VMEM((rows, width), BF16),
            pltpu.VMEM((bins, width), F32),
            pltpu.VMEM((slots, rows), BF16),
            pltpu.VMEM(pair_proj.shape, BF16),
            pltpu.VMEM(donor_w.shape, BF16),
            pltpu.VMEM((n_col, 1, listed), jnp.int32),
            pltpu.VMEM((n_col, 1, listed), jnp.int32),
            pltpu.VMEM((bins, lanes), F32),
            pltpu.VMEM((bins, lanes), F32),
            pltpu.VMEM((n_col, CAP, lanes), BF16),
            dma((2,)),
            dma((3,)),
            dma((chunks, 3)),
            dma((2,)),
            dma((2,)),
            dma((2,)),
            dma((n_col - 1,)),
            dma((n_col - 1,)),
            dma((n_col - 1,)),
            dma((n_col - 1,)),
            dma((n_col - 1,)),
            dma((n_col - 1,)),
            dma((n_col - 1,)),
            dma((n_col - 1,)),
            dma((n_row,)),
            dma((n_row,)),
        ],
        compiler_params=pltpu.CompilerParams(
            collective_id=0, has_side_effects=True, vmem_limit_bytes=56 * 1024 * 1024
        ),
        name="trunk",
    )(
        sequence,
        filter_weight,
        pair_proj,
        donor_w,
        pair_out,
        donor_pos.reshape(1, listed),
        acceptor_bin.reshape(1, listed),
    )
    done = [pltpu.with_memory_space_constraint(a, pltpu.VMEM) for a in done]
    return pl.pallas_call(
        leave,
        out_shape=(
            jax.ShapeDtypeStruct((tile_rows, tile_cols, lanes), BF16),
            jax.ShapeDtypeStruct((slots, lanes), BF16),
        ),
        in_specs=[vmem] * 2,
        out_specs=(hbm, hbm),
        scratch_shapes=[dma((2,))],
        name="leave",
    )(*done)


def solution(mesh):
    placed = (P(("row", "col"), None), P(), P(), P(), P(), P(("row", "col")), P(("row", "col")))
    return jax.shard_map(
        functools.partial(local, mesh.shape["row"], mesh.shape["col"]),
        mesh=mesh,
        in_specs=placed,
        out_specs=(P("row", "col", None), P(("row", "col"), None)),
        check_vma=False,
    )
```

```python
import functools

import jax
import jax.numpy as jnp
from jax import lax
from jax.experimental import pallas as pl
from jax.experimental.pallas import tpu as pltpu
from jax.sharding import PartitionSpec as P

DILATION_STEP = 32
POOL = 128
CAP = 64
LANES = 128
CHUNK = 256
AHEAD = 3
NEAR = 0.75
FAR = 1.5
MESH = pl.DeviceIdType.MESH
F32 = jnp.float32
BF16 = jnp.bfloat16


def dot(a, b):
    return jnp.dot(a, b, preferred_element_type=F32)


def dot_rows(a, b):
    return lax.dot_general(a, b, (((1,), (1,)), ((), ())), preferred_element_type=F32)


def hot(condition):
    return jnp.where(condition, 1.0, 0.0)


def trunk(
    n_row,
    n_col,
    x_hbm,
    w_hbm,
    proj_hbm,
    donor_hbm,
    out_hbm,
    pos_hbm,
    bin_hbm,
    pair_out,
    junction_out,
    rows_out,
    cols_out,
    emb_out,
    weight_out,
    xbuf,
    wbuf,
    mixed,
    parts,
    kept,
    hidden,
    pooled,
    select,
    proj_ref,
    donor_ref,
    pos_list,
    bin_list,
    row_send,
    col_send,
    emb_send,
    x_sem,
    end_sem,
    w_sem,
    list_sem,
    halo_send_sem,
    halo_recv_sem,
    pos_send_sem,
    pos_recv_sem,
    bin_send_sem,
    bin_recv_sem,
    emb_send_sem,
    emb_recv_sem,
    row_send_sem,
    row_recv_sem,
    col_send_sem,
    col_recv_sem,
):
    rows, width = x_hbm.shape
    step = DILATION_STEP
    chunks = width // CHUNK
    bins = rows // POOL
    tile_cols = bins * n_row
    slots = n_col * CAP
    listed = pos_hbm.shape[1]
    count = n_row * n_col
    my_row = lax.axis_index("row")
    my_col = lax.axis_index("col")
    me = my_row * n_col + my_col

    groups = rows // POOL
    blocks = POOL // step

    def place(flat):
        return (flat // n_col, lax.rem(flat, n_col))

    def w_copy(tap, n):
        return pltpu.make_async_copy(
            w_hbm.at[tap, :, pl.ds(pl.multiple_of(n * CHUNK, CHUNK), CHUNK)], wbuf.at[n, tap], w_sem.at[n, tap]
        )

    half = rows // 2

    def x_copy(index):
        return pltpu.make_async_copy(
            x_hbm.at[pl.ds(index * half, half)], xbuf.at[pl.ds(step + index * half, half)], x_sem.at[index]
        )

    pos_copy = pltpu.make_async_copy(pos_hbm, pos_list.at[my_col], list_sem.at[0])
    bin_copy = pltpu.make_async_copy(bin_hbm, bin_list.at[my_col], list_sem.at[1])
    proj_copy = pltpu.make_async_copy(proj_hbm, proj_ref, end_sem.at[0])
    donor_copy = pltpu.make_async_copy(donor_hbm, donor_ref, end_sem.at[1])
    weight_copy = pltpu.make_async_copy(out_hbm, weight_out, end_sem.at[2])
    pos_copy.start()
    bin_copy.start()
    x_copy(0).start()
    x_copy(1).start()

    has_left = me > 0
    has_right = me < count - 1
    col_home = me // n_row
    self_col = col_home == my_col
    barrier = pltpu.get_barrier_semaphore()

    @pl.when(has_left)
    def _():
        pl.semaphore_signal(barrier, inc=1, device_id=place(me - 1), device_id_type=MESH)

    @pl.when(has_right)
    def _():
        pl.semaphore_signal(barrier, inc=1, device_id=place(me + 1), device_id_type=MESH)

    for d in range(1, n_col):
        pl.semaphore_signal(barrier, inc=1, device_id=(my_row, lax.rem(my_col + d, n_col)), device_id_type=MESH)
    for i in range(n_row):
        source = my_col * n_row + i

        @pl.when(source != me)
        def _():
            pl.semaphore_signal(barrier, inc=1, device_id=place(source), device_id_type=MESH)


    pos_copy.wait()
    bin_copy.wait()
    for tap in range(3):
        w_copy(tap, 0).start()
    before = lax.broadcasted_iota(jnp.int32, (listed, listed), 0) < lax.broadcasted_iota(jnp.int32, (listed, listed), 1)
    before = hot(before).astype(BF16)
    kinds = max(16, n_col)
    kind = lax.broadcasted_iota(jnp.int32, (kinds, listed), 0)

    def group_of(acceptor):
        group = jnp.zeros_like(acceptor)
        for k in range(1, n_col):
            group = group + jnp.where(acceptor >= k * tile_cols, 1, 0)
        return group

    pos = pos_list[my_col]
    group = group_of(bin_list[my_col])
    in_group = hot(kind == group)
    rank = jnp.sum(in_group * dot(in_group.astype(BF16), before), axis=0, keepdims=True)
    slot = group.astype(F32) * float(CAP) + rank
    slot_hot = hot(lax.broadcasted_iota(jnp.int32, (slots, listed), 0).astype(F32) == slot).astype(BF16)
    within = pos % POOL
    held = (within // step) * (groups * step) + (pos // POOL) * step + within % step
    pos_hot = hot(lax.broadcasted_iota(jnp.int32, (rows, listed), 0) == held).astype(BF16)
    select[...] = dot_rows(slot_hot, pos_hot).astype(BF16)

    def up_copy():
        return pltpu.make_async_remote_copy(
            src_ref=x_hbm.at[pl.ds(0, step)],
            dst_ref=xbuf.at[pl.ds(rows + step, step)],
            send_sem=halo_send_sem.at[0],
            recv_sem=halo_recv_sem.at[0],
            device_id=place(me - 1),
            device_id_type=MESH,
        )

    def down_copy():
        return pltpu.make_async_remote_copy(
            src_ref=x_hbm.at[pl.ds(rows - step, step)],
            dst_ref=xbuf.at[pl.ds(0, step)],
            send_sem=halo_send_sem.at[1],
            recv_sem=halo_recv_sem.at[1],
            device_id=place(me + 1),
            device_id_type=MESH,
        )

    def row_group_copies(src, dst, send_sem, recv_sem, whole):
        copies = []
        for d in range(1, n_col):
            there = lax.rem(my_col + d, n_col)
            copies.append(
                pltpu.make_async_remote_copy(
                    src_ref=src if whole else src.at[there],
                    dst_ref=dst.at[my_col],
                    send_sem=send_sem.at[d - 1],
                    recv_sem=recv_sem.at[d - 1],
                    device_id=(my_row, there),
                    device_id_type=MESH,
                )
            )
        return copies

    def row_group_arrivals(src, dst, send_sem, recv_sem):
        for d in range(1, n_col):
            source = lax.rem(my_col + n_col - d, n_col)
            pltpu.make_async_remote_copy(
                src_ref=src,
                dst_ref=dst.at[source],
                send_sem=send_sem.at[d - 1],
                recv_sem=recv_sem.at[d - 1],
                device_id=(my_row, source),
                device_id_type=MESH,
            ).wait_recv()

    @pl.when(jnp.logical_not(has_left))
    def _():
        xbuf[0:step] = jnp.zeros((step, width), BF16)

    @pl.when(jnp.logical_not(has_right))
    def _():
        xbuf[rows + step : rows + 2 * step] = jnp.zeros((step, width), BF16)

    near, far = NEAR * NEAR, FAR * FAR

    def block(group, k, cols):
        start = group * POOL + k * step
        return xbuf[start : start + step, cols].astype(F32)

    def put(k, group, cols, value):
        parts[k, group * step : (group + 1) * step, cols] = value.astype(BF16)

    def combine_inner(group, cols):
        one, two, three, four = (block(group, k, cols) for k in range(1, 5))
        by_near, by_far = 0.25 / (near * (near - far)), 0.25 / (far * (far - near))
        even = by_near * four - (by_near * far) * two
        odd = (NEAR * by_near) * three - (NEAR * by_near * far) * one
        put(1, group, cols, even + odd)
        put(2, group, cols, even - odd)
        even = by_far * four - (by_far * near) * two
        odd = (FAR * by_far) * three - (FAR * by_far * near) * one
        put(3, group, cols, even + odd)
        put(4, group, cols, even - odd)

    def combine_first(group, cols):
        zero, two, four = (block(group, k, cols) for k in (0, 2, 4))
        put(0, group, cols, 0.5 * zero - (0.5 * (near + far) / (near * far)) * two + (0.5 / (near * far)) * four)

    def combine_last(group, cols):
        one, three, five = (block(group, k, cols) for k in (1, 3, 5))
        put(5, group, cols, 0.5 * five - (0.5 * (near + far)) * three + (0.5 * near * far) * one)

    everything = slice(0, width)
    x_copy(0).wait()
    for group in range(groups // 2):
        for start in range(0, width, 128):
            combine_inner(group, slice(start, start + 128))
    x_copy(1).wait()
    for n in range(1, AHEAD):
        for tap in range(3):
            w_copy(tap, n).start()
    for group in range(groups // 2, groups):
        for start in range(0, width, 128):
            combine_inner(group, slice(start, start + 128))

    def mix(n):
        def scaled(value, by):
            return value * jnp.asarray(by, BF16)

        first, second, third = wbuf[n, 0], scaled(wbuf[n, 1], NEAR), scaled(wbuf[n, 2], near)
        outer = first + third
        mixed[0] = outer + second
        mixed[1] = outer - second
        outer = first + scaled(third, far / near)
        second = scaled(second, FAR / NEAR)
        mixed[2] = outer + second
        mixed[3] = outer - second

    def finish(k, value, cols):
        value = value + value * jnp.tanh(value)
        sums = []
        for group in range(groups):
            start = group * POOL + k * step
            out = xbuf[step + start : step + start + step, cols].astype(F32) + value[group * step : (group + 1) * step]
            sums.append(out)
            start = (k * groups + group) * step
            hidden[start : start + step, cols] = out.astype(BF16)
        return sums

    def pool(first, second):
        return jnp.concatenate([jnp.sum(a + b, axis=0, keepdims=True) for a, b in zip(first, second)], axis=0)

    def first_pass(n, carry):
        cols = pl.ds(pl.multiple_of(n * CHUNK, CHUNK), CHUNK)
        for tap in range(3):
            w_copy(tap, n).wait()

        @pl.when(n + AHEAD < chunks)
        def _():
            for tap in range(3):
                w_copy(tap, n + AHEAD).start()

        mix(n)
        plus, minus = dot(parts[1], mixed[0]), dot(parts[2], mixed[1])
        near_sum, near_gap = plus + minus, plus - minus
        plus, minus = dot(parts[3], mixed[2]), dot(parts[4], mixed[3])
        far_sum, far_gap = plus + minus, plus - minus
        kept[0, :, cols] = near_sum + far_sum
        kept[1, :, cols] = (NEAR * near) * near_gap + (FAR * far) * far_gap
        second = finish(1, NEAR * near_gap + FAR * far_gap, cols)
        third = finish(2, near * near_sum + far * far_sum, cols)
        pooled[:, cols] = pool(second, third)
        for group in range(groups):
            if group > 0:
                combine_first(group, cols)
            if group < groups - 1:
                combine_last(group, cols)
        return carry

    neighbours = jnp.where(has_left, 1, 0) + jnp.where(has_right, 1, 0)
    pl.semaphore_wait(barrier, neighbours + n_col - 1 + n_row - jnp.where(self_col, 1, 0))

    @pl.when(has_left)
    def _():
        up_copy().start()

    @pl.when(has_right)
    def _():
        down_copy().start()

    list_copies = row_group_copies(pos_hbm, pos_list, pos_send_sem, pos_recv_sem, True)
    list_copies += row_group_copies(bin_hbm, bin_list, bin_send_sem, bin_recv_sem, True)
    for copy in list_copies:
        copy.start()

    donor_copy.start()
    proj_copy.start()
    weight_copy.start()
    lax.fori_loop(0, chunks, first_pass, 0)

    @pl.when(has_left)
    def _():
        down_copy().wait_recv()

    @pl.when(has_right)
    def _():
        up_copy().wait_recv()

    combine_first(0, everything)
    combine_last(groups - 1, everything)

    donor_copy.wait()
    proj_copy.wait()
    weight_copy.wait()
    quarter = rows // blocks
    inner = slice(quarter, rows - quarter)

    def donor(held, n):
        cols = slice(n * CHUNK, (n + 1) * CHUNK)
        return dot(hidden[held, cols], donor_ref[cols])

    emb_inner = emb_first = emb_last = projected = square = 0.0
    for n in range(chunks):
        cols = slice(n * CHUNK, (n + 1) * CHUNK)
        first = finish(0, kept[0, :, cols] + dot(parts[0], wbuf[n, 0]), cols)
        fourth = finish(blocks - 1, kept[1, :, cols] + dot(parts[5], wbuf[n, 2]), cols)
        emb_inner += donor(inner, n)
        means = (pooled[:, cols] + pool(first, fourth)) * (1.0 / POOL)
        square += jnp.sum(means * means, axis=-1, keepdims=True)
        projected += dot(means.astype(BF16), proj_ref[cols])
        if n < chunks - 1:
            emb_first += donor(slice(0, quarter), n)
            emb_last += donor(slice(rows - quarter, rows), n)
    projected = (projected * lax.rsqrt(square * (1.0 / width) + 1e-06)).astype(BF16).astype(F32)
    row_send[...] = projected[:, :LANES]
    col_send[...] = projected[:, LANES:]

    my_slot = me - col_home * n_row

    def col_copy(r):
        return pltpu.make_async_remote_copy(
            src_ref=col_send,
            dst_ref=cols_out.at[my_slot],
            send_sem=col_send_sem.at[r],
            recv_sem=col_recv_sem.at[my_slot],
            device_id=(r, col_home),
            device_id_type=MESH,
        )

    def is_other(r):
        return jnp.logical_or(jnp.logical_not(self_col), my_row != r)

    for r in range(n_row):

        @pl.when(is_other(r))
        def _():
            col_copy(r).start()

    row_copies = row_group_copies(row_send, rows_out, row_send_sem, row_recv_sem, True)
    for copy in row_copies:
        copy.start()

    emb_first += donor(slice(0, quarter), chunks - 1)
    emb_last += donor(slice(rows - quarter, rows), chunks - 1)
    donor_emb = jnp.concatenate([emb_first, emb_inner, emb_last], axis=0).astype(BF16)
    emb_send[...] = dot(select[...], donor_emb).astype(BF16).reshape(n_col, CAP, LANES)
    emb_copies = row_group_copies(emb_send, emb_out, emb_send_sem, emb_recv_sem, False)
    for copy in emb_copies:
        copy.start()
    emb_out[my_col] = emb_send[my_col]
    rows_out[my_col] = row_send[...]

    @pl.when(self_col)
    def _():
        cols_out[my_slot] = col_send[...]

    row_group_arrivals(pos_hbm, pos_list, pos_send_sem, pos_recv_sem)
    row_group_arrivals(bin_hbm, bin_list, bin_send_sem, bin_recv_sem)
    col_lanes = -(-tile_cols // LANES) * LANES
    mine = jnp.zeros((kinds, listed), F32)
    for k in range(n_col):
        mine = jnp.where((kind == k) & (group_of(bin_list[k]) == my_col), 1.0, mine)
    ranks = dot(mine.astype(BF16), before)
    ranks = jnp.where(mine > 0.0, ranks, -1.0)
    at = lax.broadcasted_iota(jnp.int32, (CAP, listed), 0).astype(F32)
    col_at = lax.broadcasted_iota(jnp.int32, (col_lanes, listed), 0)
    row_at = lax.broadcasted_iota(jnp.int32, (LANES, listed), 0) * POOL
    col_coords, row_coords = [], []
    for k in range(n_col):
        here = hot(at == ranks[k : k + 1]).astype(BF16)
        pair_col = bin_list[k] - my_col * tile_cols
        where = pos_list[k]
        col_hot = hot(col_at == pair_col).astype(BF16)
        row_hot = hot((where >= row_at) & (where < row_at + POOL)).astype(BF16)
        coord = dot_rows(here, jnp.concatenate([col_hot, row_hot], axis=0)).astype(BF16)
        col_coords.append(coord[:, :tile_cols])
        row_coords.append(coord[:, col_lanes : col_lanes + bins])

    row_group_arrivals(row_send, rows_out, row_send_sem, row_recv_sem)
    for i in range(n_row):
        source = my_col * n_row + i

        @pl.when(source != me)
        def _():
            pltpu.make_async_remote_copy(
                src_ref=col_send,
                dst_ref=cols_out.at[i],
                send_sem=col_send_sem.at[i],
                recv_sem=col_recv_sem.at[i],
                device_id=place(source),
                device_id_type=MESH,
            ).wait_recv()

    tile_rows = bins * n_col
    weight = weight_out[...]
    row_side = rows_out[...].reshape(tile_rows, LANES)
    col_side = cols_out[...].reshape(tile_cols, LANES)
    side = min(8, tile_rows)
    for i in range(tile_rows // side):
        part = slice(i * side, (i + 1) * side)
        sums = jnp.maximum(row_side[part, None, :] + col_side[None, :, :], 0.0).astype(BF16)
        pair_out[part] = dot(sums.reshape(side * tile_cols, LANES), weight).astype(BF16).reshape(side, tile_cols, LANES)
    by_col = dot(jnp.concatenate(col_coords, axis=0), col_side.astype(BF16))
    by_row = [dot(row_coords[k], rows_out[k].astype(BF16)) for k in range(n_col)]
    sums = jnp.maximum(jnp.concatenate(by_row, axis=0) + by_col, 0.0).astype(BF16)
    looked = dot(sums, weight).astype(BF16).astype(F32)

    row_group_arrivals(emb_send.at[0], emb_out, emb_send_sem, emb_recv_sem)
    junction_out[...] = jnp.maximum(emb_out[...].reshape(slots, LANES).astype(F32) + looked, 0.0).astype(BF16)

    for copy in list_copies + row_copies + emb_copies:
        copy.wait_send()
    for r in range(n_row):

        @pl.when(is_other(r))
        def _():
            col_copy(r).wait_send()

    @pl.when(has_left)
    def _():
        up_copy().wait_send()

    @pl.when(has_right)
    def _():
        down_copy().wait_send()


def leave(pair_ref, junction_ref, pair_hbm, junction_hbm, sem):
    copies = [
        pltpu.make_async_copy(pair_ref, pair_hbm, sem.at[0]),
        pltpu.make_async_copy(junction_ref, junction_hbm, sem.at[1]),
    ]
    for copy in copies:
        copy.start()
    for copy in copies:
        copy.wait()


def local(n_row, n_col, sequence, filter_weight, pair_proj, pair_out, donor_w, donor_pos, acceptor_bin):
    rows, width = sequence.shape
    lanes = pair_out.shape[0]
    bins = rows // POOL
    listed = donor_pos.shape[0]
    chunks = width // CHUNK
    tile_rows, tile_cols = bins * n_col, bins * n_row
    slots = n_col * CAP
    vmem = pl.BlockSpec(memory_space=pltpu.VMEM)
    hbm = pl.BlockSpec(memory_space=pl.ANY)
    dma = pltpu.SemaphoreType.DMA
    done = pl.pallas_call(
        functools.partial(trunk, n_row, n_col),
        out_shape=(
            pltpu.VMEM((tile_rows, tile_cols, lanes), BF16),
            pltpu.VMEM((slots, lanes), BF16),
        ),
        in_specs=[hbm] * 7,
        out_specs=(vmem, vmem),
        scratch_shapes=[
            pltpu.VMEM((n_col, bins, lanes), F32),
            pltpu.VMEM((n_row, bins, lanes), F32),
            pltpu.VMEM((n_col, CAP, lanes), BF16),
            pltpu.VMEM(pair_out.shape, BF16),
            pltpu.VMEM((rows + 2 * DILATION_STEP, width), BF16),
            pltpu.VMEM((chunks, 3, width, CHUNK), BF16),
            pltpu.VMEM((4, width, CHUNK), BF16),
            pltpu.VMEM((6, rows // 4, width), BF16),
            pltpu.VMEM((2, rows // 4, width), F32),
            pltpu.VMEM((rows, width), BF16),
            pltpu.VMEM((bins, width), F32),
            pltpu.VMEM((slots, rows), BF16),
            pltpu.VMEM(pair_proj.shape, BF16),
            pltpu.VMEM(donor_w.shape, BF16),
            pltpu.VMEM((n_col, 1, listed), jnp.int32),
            pltpu.VMEM((n_col, 1, listed), jnp.int32),
            pltpu.VMEM((bins, lanes), F32),
            pltpu.VMEM((bins, lanes), F32),
            pltpu.VMEM((n_col, CAP, lanes), BF16),
            dma((2,)),
            dma((3,)),
            dma((chunks, 3)),
            dma((2,)),
            dma((2,)),
            dma((2,)),
            dma((n_col - 1,)),
            dma((n_col - 1,)),
            dma((n_col - 1,)),
            dma((n_col - 1,)),
            dma((n_col - 1,)),
            dma((n_col - 1,)),
            dma((n_col - 1,)),
            dma((n_col - 1,)),
            dma((n_row,)),
            dma((n_row,)),
        ],
        compiler_params=pltpu.CompilerParams(
            collective_id=0, has_side_effects=True, vmem_limit_bytes=56 * 1024 * 1024
        ),
        name="trunk",
    )(
        sequence,
        filter_weight,
        pair_proj,
        donor_w,
        pair_out,
        donor_pos.reshape(1, listed),
        acceptor_bin.reshape(1, listed),
    )
    done = [pltpu.with_memory_space_constraint(a, pltpu.VMEM) for a in done]
    return pl.pallas_call(
        leave,
        out_shape=(
            jax.ShapeDtypeStruct((tile_rows, tile_cols, lanes), BF16),
            jax.ShapeDtypeStruct((slots, lanes), BF16),
        ),
        in_specs=[vmem] * 2,
        out_specs=(hbm, hbm),
        scratch_shapes=[dma((2,))],
        name="leave",
    )(*done)


def solution(mesh):
    placed = (P(("row", "col"), None), P(), P(), P(), P(), P(("row", "col")), P(("row", "col")))
    return jax.shard_map(
        functools.partial(local, mesh.shape["row"], mesh.shape["col"]),
        mesh=mesh,
        in_specs=placed,
        out_specs=(P("row", "col", None), P(("row", "col"), None)),
        check_vma=False,
    )
```

```python
import functools

import jax
import jax.numpy as jnp
from jax import lax
from jax.experimental import pallas as pl
from jax.experimental.pallas import tpu as pltpu
from jax.sharding import PartitionSpec as P

DILATION_STEP = 32
POOL = 128
CAP = 64
LANES = 128
CHUNK = 256
AHEAD = 3
NEAR = 0.75
FAR = 1.5
MESH = pl.DeviceIdType.MESH
F32 = jnp.float32
BF16 = jnp.bfloat16


def dot(a, b):
    return jnp.dot(a, b, preferred_element_type=F32)


def dot_rows(a, b):
    return lax.dot_general(a, b, (((1,), (1,)), ((), ())), preferred_element_type=F32)


def hot(condition):
    return jnp.where(condition, 1.0, 0.0)


def trunk(
    n_row,
    n_col,
    x_hbm,
    w_hbm,
    proj_hbm,
    donor_hbm,
    out_hbm,
    pos_hbm,
    bin_hbm,
    pair_out,
    junction_out,
    rows_out,
    cols_out,
    emb_out,
    weight_out,
    xbuf,
    wbuf,
    mixed,
    parts,
    kept,
    hidden,
    pooled,
    select,
    proj_ref,
    donor_ref,
    pos_list,
    bin_list,
    row_send,
    col_send,
    emb_send,
    x_sem,
    end_sem,
    w_sem,
    list_sem,
    halo_send_sem,
    halo_recv_sem,
    pos_send_sem,
    pos_recv_sem,
    bin_send_sem,
    bin_recv_sem,
    emb_send_sem,
    emb_recv_sem,
    row_send_sem,
    row_recv_sem,
    col_send_sem,
    col_recv_sem,
):
    rows, width = x_hbm.shape
    step = DILATION_STEP
    chunks = width // CHUNK
    bins = rows // POOL
    tile_cols = bins * n_row
    slots = n_col * CAP
    listed = pos_hbm.shape[1]
    count = n_row * n_col
    my_row = lax.axis_index("row")
    my_col = lax.axis_index("col")
    me = my_row * n_col + my_col

    groups = rows // POOL
    blocks = POOL // step

    def place(flat):
        return (flat // n_col, lax.rem(flat, n_col))

    def w_copy(tap, n):
        return pltpu.make_async_copy(
            w_hbm.at[tap, :, pl.ds(pl.multiple_of(n * CHUNK, CHUNK), CHUNK)], wbuf.at[n, tap], w_sem.at[n, tap]
        )

    half = rows // 2

    def x_copy(index):
        return pltpu.make_async_copy(
            x_hbm.at[pl.ds(index * half, half)], xbuf.at[pl.ds(step + index * half, half)], x_sem.at[index]
        )

    pos_copy = pltpu.make_async_copy(pos_hbm, pos_list.at[my_col], list_sem.at[0])
    bin_copy = pltpu.make_async_copy(bin_hbm, bin_list.at[my_col], list_sem.at[1])
    proj_copy = pltpu.make_async_copy(proj_hbm, proj_ref, end_sem.at[0])
    donor_copy = pltpu.make_async_copy(donor_hbm, donor_ref, end_sem.at[1])
    weight_copy = pltpu.make_async_copy(out_hbm, weight_out, end_sem.at[2])
    pos_copy.start()
    bin_copy.start()
    x_copy(0).start()
    x_copy(1).start()

    has_left = me > 0
    has_right = me < count - 1
    col_home = me // n_row
    self_col = col_home == my_col
    barrier = pltpu.get_barrier_semaphore()

    @pl.when(has_left)
    def _():
        pl.semaphore_signal(barrier, inc=1, device_id=place(me - 1), device_id_type=MESH)

    @pl.when(has_right)
    def _():
        pl.semaphore_signal(barrier, inc=1, device_id=place(me + 1), device_id_type=MESH)

    for d in range(1, n_col):
        pl.semaphore_signal(barrier, inc=1, device_id=(my_row, lax.rem(my_col + d, n_col)), device_id_type=MESH)
    for i in range(n_row):
        source = my_col * n_row + i

        @pl.when(source != me)
        def _():
            pl.semaphore_signal(barrier, inc=1, device_id=place(source), device_id_type=MESH)


    pos_copy.wait()
    bin_copy.wait()
    for tap in range(3):
        w_copy(tap, 0).start()
    before = lax.broadcasted_iota(jnp.int32, (listed, listed), 0) < lax.broadcasted_iota(jnp.int32, (listed, listed), 1)
    before = hot(before).astype(BF16)
    kinds = max(16, n_col)
    kind = lax.broadcasted_iota(jnp.int32, (kinds, listed), 0)

    def group_of(acceptor):
        group = jnp.zeros_like(acceptor)
        for k in range(1, n_col):
            group = group + jnp.where(acceptor >= k * tile_cols, 1, 0)
        return group

    pos = pos_list[my_col]
    group = group_of(bin_list[my_col])
    in_group = hot(kind == group)
    rank = jnp.sum(in_group * dot(in_group.astype(BF16), before), axis=0, keepdims=True)
    slot = group.astype(F32) * float(CAP) + rank
    slot_hot = hot(lax.broadcasted_iota(jnp.int32, (slots, listed), 0).astype(F32) == slot).astype(BF16)
    within = pos % POOL
    held = (within // step) * (groups * step) + (pos // POOL) * step + within % step
    pos_hot = hot(lax.broadcasted_iota(jnp.int32, (rows, listed), 0) == held).astype(BF16)
    select[...] = dot_rows(slot_hot, pos_hot).astype(BF16)

    def up_copy():
        return pltpu.make_async_remote_copy(
            src_ref=x_hbm.at[pl.ds(0, step)],
            dst_ref=xbuf.at[pl.ds(rows + step, step)],
            send_sem=halo_send_sem.at[0],
            recv_sem=halo_recv_sem.at[0],
            device_id=place(me - 1),
            device_id_type=MESH,
        )

    def down_copy():
        return pltpu.make_async_remote_copy(
            src_ref=x_hbm.at[pl.ds(rows - step, step)],
            dst_ref=xbuf.at[pl.ds(0, step)],
            send_sem=halo_send_sem.at[1],
            recv_sem=halo_recv_sem.at[1],
            device_id=place(me + 1),
            device_id_type=MESH,
        )

    def row_group_copies(src, dst, send_sem, recv_sem, whole):
        copies = []
        for d in range(1, n_col):
            there = lax.rem(my_col + d, n_col)
            copies.append(
                pltpu.make_async_remote_copy(
                    src_ref=src if whole else src.at[there],
                    dst_ref=dst.at[my_col],
                    send_sem=send_sem.at[d - 1],
                    recv_sem=recv_sem.at[d - 1],
                    device_id=(my_row, there),
                    device_id_type=MESH,
                )
            )
        return copies

    def row_group_arrivals(src, dst, send_sem, recv_sem):
        for d in range(1, n_col):
            source = lax.rem(my_col + n_col - d, n_col)
            pltpu.make_async_remote_copy(
                src_ref=src,
                dst_ref=dst.at[source],
                send_sem=send_sem.at[d - 1],
                recv_sem=recv_sem.at[d - 1],
                device_id=(my_row, source),
                device_id_type=MESH,
            ).wait_recv()

    @pl.when(jnp.logical_not(has_left))
    def _():
        xbuf[0:step] = jnp.zeros((step, width), BF16)

    @pl.when(jnp.logical_not(has_right))
    def _():
        xbuf[rows + step : rows + 2 * step] = jnp.zeros((step, width), BF16)

    near, far = NEAR * NEAR, FAR * FAR

    def block(group, k, cols):
        start = group * POOL + k * step
        return xbuf[start : start + step, cols].astype(F32)

    def put(k, group, cols, value):
        parts[k, group * step : (group + 1) * step, cols] = value.astype(BF16)

    def combine_inner(group, cols):
        one, two, three, four = (block(group, k, cols) for k in range(1, 5))
        by_near, by_far = 0.25 / (near * (near - far)), 0.25 / (far * (far - near))
        even = by_near * four - (by_near * far) * two
        odd = (NEAR * by_near) * three - (NEAR * by_near * far) * one
        put(1, group, cols, even + odd)
        put(2, group, cols, even - odd)
        even = by_far * four - (by_far * near) * two
        odd = (FAR * by_far) * three - (FAR * by_far * near) * one
        put(3, group, cols, even + odd)
        put(4, group, cols, even - odd)

    def combine_first(group, cols):
        zero, two, four = (block(group, k, cols) for k in (0, 2, 4))
        put(0, group, cols, 0.5 * zero - (0.5 * (near + far) / (near * far)) * two + (0.5 / (near * far)) * four)

    def combine_last(group, cols):
        one, three, five = (block(group, k, cols) for k in (1, 3, 5))
        put(5, group, cols, 0.5 * five - (0.5 * (near + far)) * three + (0.5 * near * far) * one)

    x_copy(0).wait()
    for group in range(groups // 2):
        for start in range(0, width, 128):
            combine_inner(group, slice(start, start + 128))
    x_copy(1).wait()
    for n in range(1, AHEAD):
        for tap in range(3):
            w_copy(tap, n).start()
    for group in range(groups // 2, groups):
        for start in range(0, width, 128):
            combine_inner(group, slice(start, start + 128))

    def mix(n):
        def scaled(value, by):
            return value * jnp.asarray(by, BF16)

        first, second, third = wbuf[n, 0], scaled(wbuf[n, 1], NEAR), scaled(wbuf[n, 2], near)
        outer = first + third
        mixed[0] = outer + second
        mixed[1] = outer - second
        outer = first + scaled(third, far / near)
        second = scaled(second, FAR / NEAR)
        mixed[2] = outer + second
        mixed[3] = outer - second

    def finish(k, value, cols):
        value = value + value * jnp.tanh(value)
        sums = []
        for group in range(groups):
            start = group * POOL + k * step
            out = xbuf[step + start : step + start + step, cols].astype(F32) + value[group * step : (group + 1) * step]
            sums.append(out)
            start = (k * groups + group) * step
            hidden[start : start + step, cols] = out.astype(BF16)
        return sums

    def pool(first, second):
        return jnp.concatenate([jnp.sum(a + b, axis=0, keepdims=True) for a, b in zip(first, second)], axis=0)

    def first_pass(n, carry):
        cols = pl.ds(pl.multiple_of(n * CHUNK, CHUNK), CHUNK)
        for tap in range(3):
            w_copy(tap, n).wait()

        @pl.when(n + AHEAD < chunks)
        def _():
            for tap in range(3):
                w_copy(tap, n + AHEAD).start()

        mix(n)
        plus, minus = dot(parts[1], mixed[0]), dot(parts[2], mixed[1])
        near_sum, near_gap = plus + minus, plus - minus
        plus, minus = dot(parts[3], mixed[2]), dot(parts[4], mixed[3])
        far_sum, far_gap = plus + minus, plus - minus
        kept[0, :, cols] = near_sum + far_sum
        kept[1, :, cols] = (NEAR * near) * near_gap + (FAR * far) * far_gap
        second = finish(1, NEAR * near_gap + FAR * far_gap, cols)
        third = finish(2, near * near_sum + far * far_sum, cols)
        pooled[:, cols] = pool(second, third)
        for group in range(groups):
            if group > 0:
                combine_first(group, cols)
            if group < groups - 1:
                combine_last(group, cols)
        return carry

    neighbours = jnp.where(has_left, 1, 0) + jnp.where(has_right, 1, 0)
    pl.semaphore_wait(barrier, neighbours + n_col - 1 + n_row - jnp.where(self_col, 1, 0))

    @pl.when(has_left)
    def _():
        up_copy().start()

    @pl.when(has_right)
    def _():
        down_copy().start()

    list_copies = row_group_copies(pos_hbm, pos_list, pos_send_sem, pos_recv_sem, True)
    list_copies += row_group_copies(bin_hbm, bin_list, bin_send_sem, bin_recv_sem, True)
    for copy in list_copies:
        copy.start()

    donor_copy.start()
    proj_copy.start()
    weight_copy.start()
    lax.fori_loop(0, chunks, first_pass, 0)

    @pl.when(has_left)
    def _():
        down_copy().wait_recv()

    @pl.when(has_right)
    def _():
        up_copy().wait_recv()

    for start in range(0, width, LANES):
        combine_first(0, slice(start, start + LANES))
        combine_last(groups - 1, slice(start, start + LANES))

    donor_copy.wait()
    proj_copy.wait()
    weight_copy.wait()
    quarter = rows // blocks
    inner = slice(quarter, rows - quarter)

    def donor(held, n):
        cols = slice(n * CHUNK, (n + 1) * CHUNK)
        return dot(hidden[held, cols], donor_ref[cols])

    emb_inner = emb_first = emb_last = projected = square = 0.0
    for n in range(chunks):
        cols = slice(n * CHUNK, (n + 1) * CHUNK)
        first = finish(0, kept[0, :, cols] + dot(parts[0], wbuf[n, 0]), cols)
        fourth = finish(blocks - 1, kept[1, :, cols] + dot(parts[5], wbuf[n, 2]), cols)
        emb_inner += donor(inner, n)
        means = (pooled[:, cols] + pool(first, fourth)) * (1.0 / POOL)
        square += jnp.sum(means * means, axis=-1, keepdims=True)
        projected += dot(means.astype(BF16), proj_ref[cols])
        if n < chunks - 1:
            emb_first += donor(slice(0, quarter), n)
            emb_last += donor(slice(rows - quarter, rows), n)
    projected = (projected * lax.rsqrt(square * (1.0 / width) + 1e-06)).astype(BF16).astype(F32)
    row_send[...] = projected[:, :LANES]
    col_send[...] = projected[:, LANES:]

    my_slot = me - col_home * n_row

    def col_copy(r):
        return pltpu.make_async_remote_copy(
            src_ref=col_send,
            dst_ref=cols_out.at[my_slot],
            send_sem=col_send_sem.at[r],
            recv_sem=col_recv_sem.at[my_slot],
            device_id=(r, col_home),
            device_id_type=MESH,
        )

    def is_other(r):
        return jnp.logical_or(jnp.logical_not(self_col), my_row != r)

    for r in range(n_row):

        @pl.when(is_other(r))
        def _():
            col_copy(r).start()

    row_copies = row_group_copies(row_send, rows_out, row_send_sem, row_recv_sem, True)
    for copy in row_copies:
        copy.start()

    emb_first += donor(slice(0, quarter), chunks - 1)
    emb_last += donor(slice(rows - quarter, rows), chunks - 1)
    donor_emb = jnp.concatenate([emb_first, emb_inner, emb_last], axis=0).astype(BF16)
    emb_send[...] = dot(select[...], donor_emb).astype(BF16).reshape(n_col, CAP, LANES)
    emb_copies = row_group_copies(emb_send, emb_out, emb_send_sem, emb_recv_sem, False)
    for copy in emb_copies:
        copy.start()
    emb_out[my_col] = emb_send[my_col]
    rows_out[my_col] = row_send[...]

    @pl.when(self_col)
    def _():
        cols_out[my_slot] = col_send[...]

    row_group_arrivals(pos_hbm, pos_list, pos_send_sem, pos_recv_sem)
    row_group_arrivals(bin_hbm, bin_list, bin_send_sem, bin_recv_sem)
    col_lanes = -(-tile_cols // LANES) * LANES
    mine = jnp.zeros((kinds, listed), F32)
    for k in range(n_col):
        mine = jnp.where((kind == k) & (group_of(bin_list[k]) == my_col), 1.0, mine)
    ranks = dot(mine.astype(BF16), before)
    ranks = jnp.where(mine > 0.0, ranks, -1.0)
    at = lax.broadcasted_iota(jnp.int32, (CAP, listed), 0).astype(F32)
    col_at = lax.broadcasted_iota(jnp.int32, (col_lanes, listed), 0)
    row_at = lax.broadcasted_iota(jnp.int32, (LANES, listed), 0) * POOL
    col_coords, row_coords = [], []
    for k in range(n_col):
        here = hot(at == ranks[k : k + 1]).astype(BF16)
        pair_col = bin_list[k] - my_col * tile_cols
        where = pos_list[k]
        col_hot = hot(col_at == pair_col).astype(BF16)
        row_hot = hot((where >= row_at) & (where < row_at + POOL)).astype(BF16)
        coord = dot_rows(here, jnp.concatenate([col_hot, row_hot], axis=0)).astype(BF16)
        col_coords.append(coord[:, :tile_cols])
        row_coords.append(coord[:, col_lanes : col_lanes + bins])

    row_group_arrivals(row_send, rows_out, row_send_sem, row_recv_sem)
    for i in range(n_row):
        source = my_col * n_row + i

        @pl.when(source != me)
        def _():
            pltpu.make_async_remote_copy(
                src_ref=col_send,
                dst_ref=cols_out.at[i],
                send_sem=col_send_sem.at[i],
                recv_sem=col_recv_sem.at[i],
                device_id=place(source),
                device_id_type=MESH,
            ).wait_recv()

    tile_rows = bins * n_col
    weight = weight_out[...]
    row_side = rows_out[...].reshape(tile_rows, LANES)
    col_side = cols_out[...].reshape(tile_cols, LANES)
    side = min(8, tile_rows)
    for i in range(tile_rows // side):
        part = slice(i * side, (i + 1) * side)
        sums = jnp.maximum(row_side[part, None, :] + col_side[None, :, :], 0.0).astype(BF16)
        pair_out[part] = dot(sums.reshape(side * tile_cols, LANES), weight).astype(BF16).reshape(side, tile_cols, LANES)
    by_col = dot(jnp.concatenate(col_coords, axis=0), col_side.astype(BF16))
    by_row = [dot(row_coords[k], rows_out[k].astype(BF16)) for k in range(n_col)]
    sums = jnp.maximum(jnp.concatenate(by_row, axis=0) + by_col, 0.0).astype(BF16)
    looked = dot(sums, weight).astype(BF16).astype(F32)

    row_group_arrivals(emb_send.at[0], emb_out, emb_send_sem, emb_recv_sem)
    junction_out[...] = jnp.maximum(emb_out[...].reshape(slots, LANES).astype(F32) + looked, 0.0).astype(BF16)

    for copy in list_copies + row_copies + emb_copies:
        copy.wait_send()
    for r in range(n_row):

        @pl.when(is_other(r))
        def _():
            col_copy(r).wait_send()

    @pl.when(has_left)
    def _():
        up_copy().wait_send()

    @pl.when(has_right)
    def _():
        down_copy().wait_send()


def leave(pair_ref, junction_ref, pair_hbm, junction_hbm, sem):
    copies = [
        pltpu.make_async_copy(pair_ref, pair_hbm, sem.at[0]),
        pltpu.make_async_copy(junction_ref, junction_hbm, sem.at[1]),
    ]
    for copy in copies:
        copy.start()
    for copy in copies:
        copy.wait()


def local(n_row, n_col, sequence, filter_weight, pair_proj, pair_out, donor_w, donor_pos, acceptor_bin):
    rows, width = sequence.shape
    lanes = pair_out.shape[0]
    bins = rows // POOL
    listed = donor_pos.shape[0]
    chunks = width // CHUNK
    tile_rows, tile_cols = bins * n_col, bins * n_row
    slots = n_col * CAP
    vmem = pl.BlockSpec(memory_space=pltpu.VMEM)
    hbm = pl.BlockSpec(memory_space=pl.ANY)
    dma = pltpu.SemaphoreType.DMA
    done = pl.pallas_call(
        functools.partial(trunk, n_row, n_col),
        out_shape=(
            pltpu.VMEM((tile_rows, tile_cols, lanes), BF16),
            pltpu.VMEM((slots, lanes), BF16),
        ),
        in_specs=[hbm] * 7,
        out_specs=(vmem, vmem),
        scratch_shapes=[
            pltpu.VMEM((n_col, bins, lanes), F32),
            pltpu.VMEM((n_row, bins, lanes), F32),
            pltpu.VMEM((n_col, CAP, lanes), BF16),
            pltpu.VMEM(pair_out.shape, BF16),
            pltpu.VMEM((rows + 2 * DILATION_STEP, width), BF16),
            pltpu.VMEM((chunks, 3, width, CHUNK), BF16),
            pltpu.VMEM((4, width, CHUNK), BF16),
            pltpu.VMEM((6, rows // 4, width), BF16),
            pltpu.VMEM((2, rows // 4, width), F32),
            pltpu.VMEM((rows, width), BF16),
            pltpu.VMEM((bins, width), F32),
            pltpu.VMEM((slots, rows), BF16),
            pltpu.VMEM(pair_proj.shape, BF16),
            pltpu.VMEM(donor_w.shape, BF16),
            pltpu.VMEM((n_col, 1, listed), jnp.int32),
            pltpu.VMEM((n_col, 1, listed), jnp.int32),
            pltpu.VMEM((bins, lanes), F32),
            pltpu.VMEM((bins, lanes), F32),
            pltpu.VMEM((n_col, CAP, lanes), BF16),
            dma((2,)),
            dma((3,)),
            dma((chunks, 3)),
            dma((2,)),
            dma((2,)),
            dma((2,)),
            dma((n_col - 1,)),
            dma((n_col - 1,)),
            dma((n_col - 1,)),
            dma((n_col - 1,)),
            dma((n_col - 1,)),
            dma((n_col - 1,)),
            dma((n_col - 1,)),
            dma((n_col - 1,)),
            dma((n_row,)),
            dma((n_row,)),
        ],
        compiler_params=pltpu.CompilerParams(
            collective_id=0, has_side_effects=True, vmem_limit_bytes=56 * 1024 * 1024
        ),
        name="trunk",
    )(
        sequence,
        filter_weight,
        pair_proj,
        donor_w,
        pair_out,
        donor_pos.reshape(1, listed),
        acceptor_bin.reshape(1, listed),
    )
    done = [pltpu.with_memory_space_constraint(a, pltpu.VMEM) for a in done]
    return pl.pallas_call(
        leave,
        out_shape=(
            jax.ShapeDtypeStruct((tile_rows, tile_cols, lanes), BF16),
            jax.ShapeDtypeStruct((slots, lanes), BF16),
        ),
        in_specs=[vmem] * 2,
        out_specs=(hbm, hbm),
        scratch_shapes=[dma((2,))],
        name="leave",
    )(*done)


def solution(mesh):
    placed = (P(("row", "col"), None), P(), P(), P(), P(), P(("row", "col")), P(("row", "col")))
    return jax.shard_map(
        functools.partial(local, mesh.shape["row"], mesh.shape["col"]),
        mesh=mesh,
        in_specs=placed,
        out_specs=(P("row", "col", None), P(("row", "col"), None)),
        check_vma=False,
    )
```
